256 devices in a mesh: prow: 8 (over z), pcol: 32 (over x, y, core).
Axes of the slice: x: 4, y: 4, z: 8, core: 2. Of those that a mesh axis runs over, the one named last changes fastest.
Arguments:
- inverse_tiles: float32 [8192, 8192], P('pcol', 'prow'), may hold values from -6 to 6
- factor: float32 [2, 8192, 512], P(None, ('pcol', 'prow')), may hold values from -0.09375 to 0.09375
- link_factor: float32 [1, 512, 512], replicated, may hold values from -0.25 to 0.25
- diag_inverse: float32 [2, 512, 512], replicated, may hold values from -3 to 3
- ancestors: int32 [2, 8], replicated, may hold values from 0 to 15, as said below
Outputs:
- offdiag: float32 [2, 8192, 512], P(None, ('pcol', 'prow'))
- diag: float32 [2, 512, 512], P(None, 'pcol')
- link_blocks: float32 [1, 512, 512], P(None, 'pcol')
The draws below stay inside these ranges and needn't reach their ends.
Inputs may be any that keep to these rules, and one draw needn't show every extreme that they name: `ancestors`: row k lists 8 distinct stored block rows; every row lists block 15, and row 0 lists block 0.
All inputs are finite; a program needn't handle non-finite values.
Results may differ from the reference program's by a relative error of at most 0.0001.
Values sent between devices are 32-bit elements; how exact they have to be, the bound alone decides.
A program may use at most 64 MiB of HBM per device.

```python
import jax
import jax.numpy as jnp
from jax import lax

B = 512
NB = 16
NSUP = 2
MB = 8
ROWS = 8192


def draw_ancestors(key, part):
    listed = []
    for number in range(NSUP):
        scores = jax.random.permutation(jax.random.fold_in(key, 17 + number), NB - 1).astype(jnp.int32)
        if number == 0:
            scores = scores.at[0].set(-1)
        chosen = jnp.argsort(scores, stable=True)[:MB - 1].astype(jnp.int32)
        listed.append(jnp.concatenate([jnp.full((1,), NB - 1, jnp.int32), chosen]))
    return jnp.stack(listed)


def spiked(drawn, key, source, target, shards_of, factor):
    def block_of(dim):
        return (jnp.arange(drawn.shape[dim]) // (drawn.shape[dim] // shards_of)).reshape((-1,) + (1,) * (drawn.ndim - 1 - dim))

    near = jax.random.permutation(key, shards_of)[block_of(target)]
    other_side = (block_of(target) + shards_of // 2) % shards_of
    return jnp.where((block_of(source) == near) | (block_of(source) == other_side), factor * drawn, drawn)


def steps_of(rng, shape, cuts, least, top_value):
    loudness = 1.0
    for dim, parts in cuts:
        steps = jax.random.uniform(jax.random.fold_in(jax.random.fold_in(rng, 6), dim), (parts,), jnp.float32, least / len(cuts), top_value / len(cuts))
        loudness = loudness * jnp.repeat(jnp.exp(steps), shape[dim] // parts).reshape((-1,) + (1,) * (len(shape) - 1 - dim))
    return loudness


def noise(stream_key, shape, width, bound, pieces=(), kind=jnp.bfloat16):
    values = width * jax.random.normal(stream_key, shape, jnp.float32)
    if pieces:
        values = values * steps_of(stream_key, shape, pieces, -0.22, 0.18)
    return jnp.clip(values, -bound, bound).astype(kind)


def gaussian_with(stream_key, dims, spread, reach, cuts, heavy, kind=jnp.bfloat16):
    entries = spread * jax.random.normal(stream_key, dims, jnp.float32)
    if cuts:
        entries = entries * steps_of(stream_key, dims, cuts, -0.22, 0.18)
    return jnp.clip(spiked(entries, jax.random.fold_in(stream_key, 3), *heavy), -reach, reach).astype(kind)


def setup_inputs(seed: int = 0) -> dict:
    splits = jax.random.split(jax.random.key(seed), 6)
    inverse_tiles = gaussian_with(splits[0], (ROWS, ROWS), 1.0, 6.0, ((0, 32), (1, 8)), (1, 0, 32, 2.75), jnp.float32)
    factor = noise(splits[1], (NSUP, ROWS, B), (MB * B) ** -0.5, 0.09375, ((1, 256),), jnp.float32)
    link_factor = noise(splits[2], (NSUP - 1, B, B), B ** -0.5, 0.25, (), jnp.float32)
    diag_inverse = noise(splits[3], (NSUP, B, B), 0.5, 3.0, (), jnp.float32)
    ancestors = draw_ancestors(jax.random.fold_in(splits[5], 71), 0)
    return dict(inverse_tiles=inverse_tiles, factor=factor, link_factor=link_factor, diag_inverse=diag_inverse, ancestors=ancestors)


def select_rows(listed):
    block_ids = jnp.arange(NB * B, dtype=jnp.int32) // B
    return jnp.any(block_ids[:, None] == listed[None, :].astype(jnp.int32), axis=1).astype(jnp.float32)[:, None]


def product(left_part, right_part):
    return jnp.dot(left_part, right_part, precision=lax.Precision.HIGHEST, preferred_element_type=jnp.float32)


def reference(inverse_tiles, factor, link_factor, diag_inverse, ancestors):
    offdiag_list = []
    diag_list = []
    link_list = []
    prior_offdiag = None
    prior_diag = None
    for number in range(NSUP):
        keep_rows = select_rows(ancestors[number])
        masked = factor[number] * keep_rows
        applied = product(inverse_tiles, masked)
        gram_sum = product(masked.T, applied)
        if number == 0:
            result = -(keep_rows * applied)
            diag_block = diag_inverse[0] + gram_sum
        else:
            link_block = link_factor[number - 1]
            cross_sum = product(prior_offdiag.T, masked)
            result = -(keep_rows * (applied + product(prior_offdiag, link_block)))
            link_out = -(cross_sum + product(prior_diag, link_block))
            diag_block = diag_inverse[number] + gram_sum + product(cross_sum.T, link_block) - product(link_block.T, link_out)
            link_list.append(link_out)
        offdiag_list.append(result)
        diag_list.append(diag_block)
        prior_offdiag = result
        prior_diag = diag_block
    return (jnp.stack(offdiag_list), jnp.stack(diag_list), jnp.stack(link_list))
```

```python
import functools

import jax
import jax.numpy as jnp
from jax import lax
from jax.experimental import pallas as pl
from jax.experimental.pallas import tpu as pltpu
from jax.sharding import PartitionSpec as P

MESH = pl.DeviceIdType.MESH
F32 = jnp.float32
BF16 = jnp.bfloat16
CHUNKS = 4


def split(value):
    high = value.astype(BF16)
    low = (value - high.astype(F32)).astype(BF16)
    return high, low


def dot(left, right):
    return jnp.dot(left, right, preferred_element_type=F32)


def dot3(left, right):
    left_high, left_low = left
    right_high, right_low = right
    return dot(left_high, right_high) + dot(left_high, right_low) + dot(left_low, right_high)


def kernel(
    tiles_hbm, factor_ref, link_hbm, dinv_hbm, anc_ref,
    off_ref, diag_ref, link_ref,
    tiles_v, tiles_hi, tiles_lo, first, factor_z, factor_split, part, arrive, rows, pair_factor,
    link_v, link_hi, link_lo, dinv0_v, dinv1_v, extra,
    left_buf, right_buf, gram, gram_in, line, line_in, plane, z_in, total, final,
    local_sem, first_sem, spread_sem, pair_sem, one_sem, two_sem, ring_sem, rows_sem,
    gram_sem, line_sem, z_sem, final_sem, send_sem, group_send,
):
    z = lax.axis_index("prow")
    p = lax.axis_index("pcol")
    core = lax.rem(p, 2)
    x = p // 8
    y = lax.rem(p // 2, 4)
    a = x + core * (y - x)
    b = y + core * (x - y)
    block = p // 2

    def device(dest_z, dest_a, dest_b):
        dest_x = dest_a + core * (dest_b - dest_a)
        dest_y = dest_b + core * (dest_a - dest_b)
        return (dest_z, (dest_x * 4 + dest_y) * 2 + core)

    def local(src, dst, sem):
        copy = pltpu.make_async_copy(src, dst, sem)
        copy.start()
        return copy

    sent = []

    def send(src, dst, recv, target):
        copy = pltpu.make_async_remote_copy(
            src_ref=src, dst_ref=dst, send_sem=send_sem.at[len(sent)], recv_sem=recv,
            device_id=target, device_id_type=MESH,
        )
        copy.start()
        sent.append(copy)

    def send_group(src, dst, recv, target, group):
        pltpu.make_async_remote_copy(
            src_ref=src, dst_ref=dst, send_sem=group_send.at[group], recv_sem=recv,
            device_id=target, device_id_type=MESH,
        ).start()

    def wait_bytes(ref, sem):
        pltpu.make_async_copy(ref, ref, sem).wait()

    own_tiles = local(tiles_hbm, tiles_v.at[core], local_sem.at[0])
    own_link = local(link_hbm.at[0], link_v, local_sem.at[1])
    own_dinv0 = local(dinv_hbm.at[0], dinv0_v, local_sem.at[2])
    slice_rows = pl.ds(pl.multiple_of(p * 16, 16), 16)
    own_dinv1 = local(dinv_hbm.at[:, slice_rows], dinv1_v, local_sem.at[3])

    barrier = pltpu.get_barrier_semaphore()
    for step in range(1, 32):
        pl.semaphore_signal(barrier, inc=1, device_id=(z, lax.rem(p + step, 32)), device_id_type=MESH)
    for step in range(1, 8):
        for other in range(2):
            pl.semaphore_signal(
                barrier, inc=1, device_id=(lax.rem(z + step, 8), (p // 2) * 2 + other), device_id_type=MESH
            )
    pl.semaphore_wait(barrier, 31 + 14)

    partner = (z, p + 1 - 2 * core)

    def tile_of(target):
        number = lax.rem(target, 2)
        tx = target // 8
        ty = lax.rem(target // 2, 4)
        lane = tx + number * (ty - tx)
        row = ty + number * (tx - ty)
        return factor_ref.at[
            number, pl.ds(pl.multiple_of(row * 8, 8), 8), pl.ds(pl.multiple_of(lane * 128, 128), 128)
        ]

    for step in range(1, 32):
        target = lax.rem(p + step, 32)
        send_group(tile_of(target), first.at[p], first_sem, (z, target), 0)
    local(tile_of(p), first.at[p], first_sem)

    send(tiles_hbm, tiles_v.at[core], pair_sem.at[0], partner)
    send(factor_ref, pair_factor.at[core], pair_sem.at[1], partner)
    own_pair = local(factor_ref, pair_factor.at[core], local_sem.at[4])

    wait_bytes(first, first_sem)
    mine = factor_z.at[a, :, z, b]
    for step in range(1, 8):
        dest_z = lax.rem(z + step, 8)
        send_group(first.at[pl.ds(4 * dest_z, 4)], mine, spread_sem, (dest_z, p), 1)
    local(first.at[pl.ds(4 * z, 4)], mine, spread_sem)

    def keep_of(number, row_block):
        listed = anc_ref[number, 0] == row_block
        for entry in range(1, anc_ref.shape[1]):
            listed = jnp.logical_or(listed, anc_ref[number, entry] == row_block)
        return jnp.where(listed, jnp.float32(1), jnp.float32(0))

    keep_low = keep_of(core, 2 * z)
    keep_high = keep_of(core, 2 * z + 1)
    keep0 = keep_of(0, block)
    keep1 = keep_of(1, block)

    own_tiles.wait()

    def split_tiles(half):
        def go(step, carry):
            at = pl.ds(pl.multiple_of(step * 32, 32), 32)
            high, low = split(tiles_v[half, at, :])
            put = pl.ds(pl.multiple_of(half * 256 + step * 32, 32), 32)
            tiles_hi[put, :] = high
            tiles_lo[put, :] = low
            return carry

        lax.fori_loop(0, 8, go, 0)

    split_tiles(core)
    own_link.wait()
    own_dinv0.wait()
    own_dinv1.wait()

    def split_link(step, carry):
        at = pl.ds(pl.multiple_of(step * 32, 32), 32)
        high, low = split(link_v[at, :])
        link_hi[at, :] = high
        link_lo[at, :] = low
        return carry

    lax.fori_loop(0, 16, split_link, 0)

    sent[0].wait_recv()
    split_tiles(1 - core)

    def piece(lane, row):
        return factor_z.at[lane, :, :, row]

    def half(lane, row, which):
        return factor_z.at[lane, pl.ds(2 * which, 2), :, row]

    a_next, a_prev, a_far = lax.rem(a + 1, 4), lax.rem(a + 3, 4), lax.rem(a + 2, 4)
    b_next, b_prev, b_far = lax.rem(b + 1, 4), lax.rem(b + 3, 4), lax.rem(b + 2, 4)
    to_b_next, to_b_prev = device(z, a, b_next), device(z, a, b_prev)
    to_a_next, to_a_prev = device(z, a_next, b), device(z, a_prev, b)

    def along_a(row, order):
        send(piece(a, row), piece(a, row), two_sem.at[0, order], to_a_next)
        send(piece(a, row), piece(a, row), two_sem.at[1, order], to_a_prev)

    wait_bytes(piece(a, b), spread_sem)
    send(piece(a, b), piece(a, b), one_sem.at[0], to_b_next)
    send(piece(a, b), piece(a, b), one_sem.at[1], to_b_prev)
    along_a(b, 0)

    row_ids = lax.broadcasted_iota(jnp.int32, (16, 512), 0) + p * 16
    col_ids = lax.broadcasted_iota(jnp.int32, (16, 512), 1)
    pick = jnp.where(row_ids == col_ids, jnp.float32(1), jnp.float32(0)).astype(BF16)
    across = (((1,), (1,)), ((), ()))
    picked = lax.dot_general(pick, link_hi[...], across, preferred_element_type=F32) + lax.dot_general(
        pick, link_lo[...], across, preferred_element_type=F32
    )
    picked = dot3(split(picked), split(dinv0_v[...]))
    extra[...] = dot3(split(picked), (link_hi[...], link_lo[...]))

    wait_bytes(piece(a, b_prev), one_sem.at[0])
    send(half(a, b_prev, 0), half(a, b_prev, 0), one_sem.at[2], to_b_next)
    along_a(b_prev, 1)
    wait_bytes(piece(a, b_next), one_sem.at[1])
    send(half(a, b_next, 1), half(a, b_next, 1), one_sem.at[3], to_b_prev)
    along_a(b_next, 2)
    wait_bytes(half(a, b_far, 0), one_sem.at[2])
    wait_bytes(half(a, b_far, 1), one_sem.at[3])
    along_a(b_far, 3)
    row_order = (b, b_prev, b_next, b_far)

    def relay(order):
        row = row_order[order]
        wait_bytes(piece(a_prev, row), two_sem.at[0, order])
        send(half(a_prev, row, 0), half(a_prev, row, 0), two_sem.at[2, order], to_a_next)
        wait_bytes(piece(a_next, row), two_sem.at[1, order])
        send(half(a_next, row, 1), half(a_next, row, 1), two_sem.at[3, order], to_a_prev)

    def compute(number, lane):
        def prepare(step, carry):
            value = factor_z[lane, step].reshape(256, 128)
            value = value * jnp.where(step < 2, keep_low, keep_high)
            high, low = split(value)
            at = pl.ds(pl.multiple_of(step * 256, 256), 256)
            factor_split[at, 0:128] = high
            factor_split[at, 128:256] = low
            return carry

        lax.fori_loop(0, 4, prepare, 0)

        def multiply(step, carry):
            at = pl.ds(pl.multiple_of(step * 128, 128), 128)
            both = dot(tiles_hi[at, :], factor_split[...])
            result = both[:, 0:128] + both[:, 128:256] + dot(tiles_lo[at, :], factor_split[:, 0:128])
            part[number, step // 2, pl.ds(lax.rem(step, 2) * 4, 4)] = result.reshape(4, 32, 128)
            return carry

        lax.fori_loop(0, 4, multiply, 0)

    to_z_next, to_z_prev = (lax.rem(z + 1, 8), p), (lax.rem(z + 7, 8), p)

    def hops(number):
        return (4, 3) if number % 2 == 0 else (3, 4)

    def ring(number, step):
        forward, backward = hops(number)
        if step < forward:
            dest = lax.rem(z + forward - step, 8)
            if step:
                wait_bytes(arrive.at[number, step - 1], ring_sem.at[number, step - 1])
                part[number, :, dest] = part[number, :, dest] + arrive[number, step - 1]
            send(part.at[number, :, dest], arrive.at[number, step], ring_sem.at[number, step], to_z_next)
        if step < backward:
            dest = lax.rem(z + 8 - backward + step, 8)
            slot = forward + step
            if step:
                wait_bytes(arrive.at[number, slot - 1], ring_sem.at[number, slot - 1])
                part[number, :, dest] = part[number, :, dest] + arrive[number, slot - 1]
            send(part.at[number, :, dest], arrive.at[number, slot], ring_sem.at[number, slot], to_z_prev)

    def ring_end(number, lane):
        forward, _ = hops(number)
        wait_bytes(arrive.at[number, forward - 1], ring_sem.at[number, forward - 1])
        wait_bytes(arrive.at[number, 6], ring_sem.at[number, 6])
        value = part[number, :, z] + arrive[number, forward - 1] + arrive[number, 6]
        rows[core, lane] = value.reshape(64, 128)
        send(rows.at[core, lane], rows.at[core, lane], rows_sem.at[number], partner)

    compute(0, a)
    ring(0, 0)
    relay(0)
    relay(1)
    ring(0, 1)
    relay(2)
    relay(3)
    ring(0, 2)
    compute(1, a_prev)
    ring(1, 0)
    ring(0, 3)
    compute(2, a_next)
    ring(2, 0)
    ring(1, 1)
    for order in range(4):
        wait_bytes(half(a_far, row_order[order], 0), two_sem.at[2, order])
        wait_bytes(half(a_far, row_order[order], 1), two_sem.at[3, order])
    compute(3, a_far)
    ring(3, 0)
    ring(2, 1)
    ring(1, 2)
    ring_end(0, a)
    ring(3, 1)
    ring(2, 2)
    ring(1, 3)
    ring(3, 2)
    ring(2, 3)
    ring_end(1, a_prev)
    ring(3, 3)
    ring_end(2, a_next)

    own_pair.wait()
    wait_bytes(pair_factor.at[1 - core], pair_sem.at[1])

    def own_rows(number, keep):
        return jnp.concatenate([pair_factor[0, number], pair_factor[1, number]], axis=0) * keep

    masked0 = own_rows(0, keep0)
    masked1 = own_rows(1, keep1)
    link_pair = (link_hi[...], link_lo[...])
    linked0 = dot3(split(masked0), link_pair)

    def put_left(at, value):
        high, low = split(value)
        left_buf[at:at + 64, :] = high
        left_buf[at + 64:at + 128, :] = high
        left_buf[at + 128:at + 192, :] = low

    half_cols = pl.ds(pl.multiple_of(core * 256, 256), 256)

    def put_right(at, value):
        high, low = split(value)
        right_buf[at:at + 64, :] = high
        right_buf[at + 64:at + 128, :] = low
        right_buf[at + 128:at + 192, :] = high

    put_left(0, -masked0)
    put_left(384, masked1)
    put_left(768, -linked0)

    ring_end(3, a_far)
    for number in range(CHUNKS):
        wait_bytes(rows.at[1 - core, 0], rows_sem.at[number])

    def joined(number):
        return jnp.concatenate([rows[number, lane] for lane in range(4)], axis=1)

    off0 = joined(0) * (-keep0)
    total[0] = off0
    total[3] = masked1
    put_left(192, off0)
    put_right(0, total[0, :, half_cols])
    put_right(192, total[3, :, half_cols])

    flip = (((0,), (0,)), ((), ()))

    def product(mat, first_row, row_count, right_row, swap):
        def go(step, carry):
            lanes = pl.ds(pl.multiple_of(step * 128, 128), 128)
            value = lax.dot_general(
                left_buf[first_row:first_row + row_count, lanes],
                right_buf[right_row:right_row + row_count, :],
                flip, preferred_element_type=F32,
            )
            for inner in range(4):
                upper = step + swap * (inner - step)
                lower = inner + swap * (step - inner)
                gram[mat, upper, lower] = value[inner * 32:(inner + 1) * 32, :]
            return carry

        lax.fori_loop(0, 4, go, 0)

    own_first = (a, b, a)
    own_second = (b, a, b)
    next_first = (to_a_next, to_b_next, to_a_next)
    prev_first = (to_a_prev, to_b_prev, to_a_prev)

    def gram_start(mat):
        up = lax.rem(own_first[mat] + 1, 4)
        down = lax.rem(own_first[mat] + 3, 4)
        far = lax.rem(own_first[mat] + 2, 4)
        low, high = pl.ds(0, 2), pl.ds(2, 2)
        send(gram.at[mat, far, low], gram_in.at[mat, 0], gram_sem.at[mat, 0], next_first[mat])
        send(gram.at[mat, far, high], gram_in.at[mat, 1], gram_sem.at[mat, 1], prev_first[mat])
        send(gram.at[mat, up, high], gram_in.at[mat, 2], gram_sem.at[mat, 2], next_first[mat])
        send(gram.at[mat, down, low], gram_in.at[mat, 3], gram_sem.at[mat, 3], prev_first[mat])

    def gram_middle(mat):
        up = lax.rem(own_first[mat] + 1, 4)
        down = lax.rem(own_first[mat] + 3, 4)
        low, high = pl.ds(0, 2), pl.ds(2, 2)
        wait_bytes(gram_in.at[mat, 0], gram_sem.at[mat, 0])
        gram[mat, up, low] = gram[mat, up, low] + gram_in[mat, 0]
        send(gram.at[mat, up, low], gram_in.at[mat, 4], gram_sem.at[mat, 4], next_first[mat])
        wait_bytes(gram_in.at[mat, 1], gram_sem.at[mat, 1])
        gram[mat, down, high] = gram[mat, down, high] + gram_in[mat, 1]
        send(gram.at[mat, down, high], gram_in.at[mat, 5], gram_sem.at[mat, 5], prev_first[mat])

    def gram_end(mat):
        here = own_first[mat]
        low, high = pl.ds(0, 2), pl.ds(2, 2)
        wait_bytes(gram_in.at[mat, 2], gram_sem.at[mat, 2])
        wait_bytes(gram_in.at[mat, 3], gram_sem.at[mat, 3])
        wait_bytes(gram_in.at[mat, 4], gram_sem.at[mat, 4])
        wait_bytes(gram_in.at[mat, 5], gram_sem.at[mat, 5])
        line[mat, low] = gram[mat, here, low] + gram_in[mat, 3] + gram_in[mat, 4]
        line[mat, high] = gram[mat, here, high] + gram_in[mat, 2] + gram_in[mat, 5]
        for step in range(1, 4):
            other = lax.rem(own_second[mat] + step, 4)
            target = device(z, a, other) if mat != 1 else device(z, other, b)
            send(line.at[mat, other], line_in.at[mat, step - 1], line_sem.at[mat, step - 1], target)

    def line_end(mat):
        for step in range(3):
            wait_bytes(line_in.at[mat, step], line_sem.at[mat, step])
        value = line[mat, own_second[mat]] + line_in[mat, 0] + line_in[mat, 1] + line_in[mat, 2]
        for row in range(4):
            for lane in range(2):
                plane[2 * row + lane, mat] = value[row * 8:(row + 1) * 8, lane * 128:(lane + 1) * 128]

    product(0, 0, 192, 0, core)
    gram_start(0)
    product(1, 192, 192, 192, 1 - core)
    gram_start(1)

    shifted = dot3(split(off0), link_pair)
    total[1] = shifted
    put_left(576, shifted)
    inner = joined(1) + shifted
    total[2] = inner
    put_right(384, total[2, :, half_cols])
    put_right(576, total[3, :, half_cols])
    put_right(768, total[1, :, half_cols])
    product(2, 384, 576, 384, core)
    gram_start(2)

    mine_rows = pl.ds(pl.multiple_of(core * 32, 32), 32)
    off_ref[0] = total[0, mine_rows, :]
    off_ref[1] = total[2, mine_rows, :] * (-keep1)

    for mat in range(3):
        gram_middle(mat)
    for mat in range(3):
        gram_end(mat)
    for mat in range(3):
        line_end(mat)

    for step in range(1, 8):
        dest_z = lax.rem(z + step, 8)
        send_group(plane.at[dest_z], z_in.at[z], z_sem, (dest_z, p), 2)
    local(plane.at[z], z_in.at[z], z_sem)
    wait_bytes(z_in, z_sem)
    value = z_in[0]
    for other in range(1, 8):
        value = value + z_in[other]
    plane_total = final.at[8]
    final[8] = value
    owner = z // 4
    slot = lax.rem(z, 4) * 2 + core
    for step in range(1, 8):
        send_group(plane_total, final.at[slot], final_sem, (lax.rem(z + step, 8), (p // 2) * 2 + owner), 3)

    @pl.when(owner == core)
    def _():
        local(plane_total, final.at[slot], final_sem)

    @pl.when(owner != core)
    def _():
        send_group(plane_total, final.at[slot], final_sem, partner, 4)

    wait_bytes(final.at[pl.ds(0, 8)], final_sem)

    def slice_of(mat):
        tiles = []
        for row in range(2):
            lanes = [final[(2 * row + lane) * 2 + side, mat] for side in range(2) for lane in range(2)]
            tiles.append(jnp.concatenate(lanes, axis=1))
        return jnp.concatenate(tiles, axis=0)

    diag0 = dinv1_v[0] + slice_of(0)
    diag_ref[0] = diag0
    link_ref[0] = -(slice_of(1) + dot3(split(diag0), (link_hi[...], link_lo[...])))
    diag_ref[1] = dinv1_v[1] + extra[...] + slice_of(2)

    for copy in sent:
        copy.wait_send()
    wait_bytes(first.at[pl.ds(0, 31)], group_send.at[0])
    wait_bytes(first.at[pl.ds(0, 28)], group_send.at[1])
    wait_bytes(plane.at[pl.ds(0, 7)], group_send.at[2])
    wait_bytes(plane.at[pl.ds(0, 7)], group_send.at[3])

    @pl.when(owner != core)
    def _():
        wait_bytes(plane.at[0], group_send.at[4])


def body(inverse_tiles, factor, link_factor, diag_inverse, ancestors):
    anywhere = pl.BlockSpec(memory_space=pl.ANY)
    vmem = pl.BlockSpec(memory_space=pltpu.VMEM)
    dma = pltpu.SemaphoreType.DMA
    return pl.pallas_call(
        kernel,
        out_shape=(
            jax.ShapeDtypeStruct((2, 32, 512), F32),
            jax.ShapeDtypeStruct((2, 16, 512), F32),
            jax.ShapeDtypeStruct((1, 16, 512), F32),
        ),
        in_specs=[anywhere, vmem, anywhere, anywhere, pl.BlockSpec(memory_space=pltpu.SMEM)],
        out_specs=(vmem, vmem, vmem),
        scratch_shapes=[
            pltpu.VMEM((2, 256, 1024), F32),
            pltpu.VMEM((512, 1024), BF16),
            pltpu.VMEM((512, 1024), BF16),
            pltpu.VMEM((32, 8, 128), F32),
            pltpu.VMEM((4, 4, 8, 4, 8, 128), F32),
            pltpu.VMEM((1024, 256), BF16),
            pltpu.VMEM((CHUNKS, 2, 8, 32, 128), F32),
            pltpu.VMEM((CHUNKS, 7, 2, 32, 128), F32),
            pltpu.VMEM((2, 4, 64, 128), F32),
            pltpu.VMEM((2, 2, 32, 512), F32),
            pltpu.VMEM((512, 512), F32),
            pltpu.VMEM((512, 512), BF16),
            pltpu.VMEM((512, 512), BF16),
            pltpu.VMEM((512, 512), F32),
            pltpu.VMEM((2, 16, 512), F32),
            pltpu.VMEM((16, 512), F32),
            pltpu.VMEM((960, 512), BF16),
            pltpu.VMEM((960, 256), BF16),
            pltpu.VMEM((3, 4, 4, 32, 256), F32),
            pltpu.VMEM((3, 6, 2, 32, 256), F32),
            pltpu.VMEM((3, 4, 32, 256), F32),
            pltpu.VMEM((3, 3, 32, 256), F32),
            pltpu.VMEM((8, 3, 8, 128), F32),
            pltpu.VMEM((8, 3, 8, 128), F32),
            pltpu.VMEM((4, 64, 512), F32),
            pltpu.VMEM((9, 3, 8, 128), F32),
            dma((5,)),
            dma,
            dma,
            dma((2,)),
            dma((4,)),
            dma((4, 4)),
            dma((CHUNKS, 7)),
            dma((CHUNKS,)),
            dma((3, 6)),
            dma((3, 3)),
            dma,
            dma,
            dma((96,)),
            dma((5,)),
        ],
        compiler_params=pltpu.CompilerParams(
            collective_id=0, has_side_effects=True, vmem_limit_bytes=48 * 1024 * 1024
        ),
    )(inverse_tiles, factor, link_factor, diag_inverse, ancestors)


def solution(mesh):
    in_specs = (P("pcol", "prow"), P(None, ("pcol", "prow"), None), P(), P(), P())
    out_specs = (P(None, ("pcol", "prow"), None), P(None, "pcol", None), P(None, "pcol", None))
    return jax.shard_map(body, mesh=mesh, in_specs=in_specs, out_specs=out_specs, check_vma=False)
```

```python
import functools

import jax
import jax.numpy as jnp
from jax import lax
from jax.experimental import pallas as pl
from jax.experimental.pallas import tpu as pltpu
from jax.sharding import PartitionSpec as P

MESH = pl.DeviceIdType.MESH
F32 = jnp.float32
BF16 = jnp.bfloat16
CHUNKS = 4
RING8 = (4, 3, 5, 2, 6, 1, 7)
PLANE = sorted(
    ((dx, dy, dc) for dx in range(4) for dy in range(4) for dc in range(2) if dx or dy or dc),
    key=lambda at: -(min(at[0], 4 - at[0]) + min(at[1], 4 - at[1]) + 0.5 * at[2]),
)


def split(value):
    high = value.astype(BF16)
    low = (value - high.astype(F32)).astype(BF16)
    return high, low


def dot(left, right):
    return jnp.dot(left, right, preferred_element_type=F32)


def dot3(left, right):
    left_high, left_low = left
    right_high, right_low = right
    return dot(left_high, right_high) + dot(left_high, right_low) + dot(left_low, right_high)


def kernel(
    tiles_hbm, factor_hbm, link_hbm, dinv_hbm, anc_hbm,
    off_ref, diag_ref, link_ref,
    anc_ref, tiles_v, tiles_hi, tiles_lo, first, factor_z, factor_split, part, arrive, rows, pair_factor,
    link_v, link_hi, link_lo, dinv0_v, dinv1_v, extra,
    left_buf, right_buf, gram, gram_in, line, line_in, plane, z_in, total, final,
    local_sem, first_sem, spread_sem, pair_sem, one_sem, two_sem, ring_sem, rows_sem,
    gram_sem, line_sem, z_sem, final_sem, send_sem, group_send,
):
    z = lax.axis_index("prow")
    p = lax.axis_index("pcol")
    core = lax.rem(p, 2)
    x = p // 8
    y = lax.rem(p // 2, 4)
    a = x + core * (y - x)
    b = y + core * (x - y)
    block = p // 2

    def device(dest_z, dest_a, dest_b):
        dest_x = dest_a + core * (dest_b - dest_a)
        dest_y = dest_b + core * (dest_a - dest_b)
        return (dest_z, (dest_x * 4 + dest_y) * 2 + core)

    def local(src, dst, sem):
        copy = pltpu.make_async_copy(src, dst, sem)
        copy.start()
        return copy

    sent = []

    def send(src, dst, recv, target):
        copy = pltpu.make_async_remote_copy(
            src_ref=src, dst_ref=dst, send_sem=send_sem.at[len(sent)], recv_sem=recv,
            device_id=target, device_id_type=MESH,
        )
        copy.start()
        sent.append(copy)

    def send_group(src, dst, recv, target, group):
        pltpu.make_async_remote_copy(
            src_ref=src, dst_ref=dst, send_sem=group_send.at[group], recv_sem=recv,
            device_id=target, device_id_type=MESH,
        ).start()

    def wait_bytes(ref, sem):
        pltpu.make_async_copy(ref, ref, sem).wait()

    own_pair = local(factor_hbm, pair_factor.at[core], local_sem.at[4])
    own_anc = local(anc_hbm, anc_ref, local_sem.at[5])
    own_tiles = local(tiles_hbm, tiles_v.at[core], local_sem.at[0])
    own_link = local(link_hbm.at[0], link_v, local_sem.at[1])
    own_dinv0 = local(dinv_hbm.at[0], dinv0_v, local_sem.at[2])
    slice_rows = pl.ds(pl.multiple_of(p * 16, 16), 16)
    own_dinv1 = local(dinv_hbm.at[:, slice_rows], dinv1_v, local_sem.at[3])

    barrier = pltpu.get_barrier_semaphore()
    def in_plane(offset):
        dx, dy, dc = offset
        return lax.rem(x + dx, 4) * 8 + lax.rem(y + dy, 4) * 2 + (1 - core if dc else core)

    for offset in PLANE:
        pl.semaphore_signal(barrier, inc=1, device_id=(z, in_plane(offset)), device_id_type=MESH)
    for step in RING8:
        for other in range(2):
            pl.semaphore_signal(
                barrier, inc=1, device_id=(lax.rem(z + step, 8), (p // 2) * 2 + other), device_id_type=MESH
            )
    pl.semaphore_wait(barrier, 31 + 14)

    partner = (z, p + 1 - 2 * core)

    def tile_of(target):
        number = lax.rem(target, 2)
        tx = target // 8
        ty = lax.rem(target // 2, 4)
        lane = tx + number * (ty - tx)
        row = ty + number * (tx - ty)
        return pair_factor.at[
            core, number, pl.ds(pl.multiple_of(row * 8, 8), 8), pl.ds(pl.multiple_of(lane * 128, 128), 128)
        ]

    own_pair.wait()
    for offset in PLANE:
        target = in_plane(offset)
        send_group(tile_of(target), first.at[p], first_sem, (z, target), 0)
    local(tile_of(p), first.at[p], first_sem)

    send(tiles_hbm, tiles_v.at[core], pair_sem.at[0], partner)
    send(pair_factor.at[core], pair_factor.at[core], pair_sem.at[1], partner)

    def keep_of(number, row_block):
        listed = anc_ref[number, 0] == row_block
        for entry in range(1, anc_ref.shape[1]):
            listed = jnp.logical_or(listed, anc_ref[number, entry] == row_block)
        return jnp.where(listed, jnp.float32(1), jnp.float32(0))

    own_anc.wait()
    keep_low = keep_of(core, 2 * z)
    keep_high = keep_of(core, 2 * z + 1)
    keep0 = keep_of(0, block)
    keep1 = keep_of(1, block)

    own_tiles.wait()

    def split_tiles(half):
        def go(step, carry):
            at = pl.ds(pl.multiple_of(step * 32, 32), 32)
            high, low = split(tiles_v[half, at, :])
            put = pl.ds(pl.multiple_of(half * 256 + step * 32, 32), 32)
            tiles_hi[put, :] = high
            tiles_lo[put, :] = low
            return carry

        lax.fori_loop(0, 8, go, 0)

    split_tiles(core)
    own_link.wait()
    own_dinv0.wait()
    own_dinv1.wait()

    def split_link(step, carry):
        at = pl.ds(pl.multiple_of(step * 32, 32), 32)
        high, low = split(link_v[at, :])
        link_hi[at, :] = high
        link_lo[at, :] = low
        return carry

    lax.fori_loop(0, 16, split_link, 0)

    row_ids = lax.broadcasted_iota(jnp.int32, (16, 512), 0) + p * 16
    col_ids = lax.broadcasted_iota(jnp.int32, (16, 512), 1)
    pick = jnp.where(row_ids == col_ids, jnp.float32(1), jnp.float32(0)).astype(BF16)
    across = (((1,), (1,)), ((), ()))
    picked = lax.dot_general(pick, link_hi[...], across, preferred_element_type=F32) + lax.dot_general(
        pick, link_lo[...], across, preferred_element_type=F32
    )
    picked = dot3(split(picked), split(dinv0_v[...]))
    extra[...] = dot3(split(picked), (link_hi[...], link_lo[...]))

    wait_bytes(first, first_sem)
    mine = factor_z.at[a, b, :, z]
    for step in RING8:
        dest_z = lax.rem(z + step, 8)
        send_group(first.at[pl.ds(4 * dest_z, 4)], mine, spread_sem, (dest_z, p), 1)
    local(first.at[pl.ds(4 * z, 4)], mine, spread_sem)

    sent[0].wait_recv()
    split_tiles(1 - core)

    wait_bytes(pair_factor.at[1 - core], pair_sem.at[1])

    def own_rows(number, keep):
        return jnp.concatenate([pair_factor[0, number], pair_factor[1, number]], axis=0) * keep

    masked0 = own_rows(0, keep0)
    masked1 = own_rows(1, keep1)
    link_pair = (link_hi[...], link_lo[...])
    linked0 = dot3(split(masked0), link_pair)

    def put_left(at, value):
        high, low = split(value)
        left_buf[at:at + 64, :] = high
        left_buf[at + 64:at + 128, :] = high
        left_buf[at + 128:at + 192, :] = low

    half_cols = pl.ds(pl.multiple_of(core * 256, 256), 256)

    def put_right(at, value):
        high, low = split(value)
        right_buf[at:at + 64, :] = high
        right_buf[at + 64:at + 128, :] = low
        right_buf[at + 128:at + 192, :] = high

    put_left(0, -masked0)
    put_left(384, masked1)
    put_left(768, -linked0)


    def piece(lane, row):
        return factor_z.at[lane, row]

    def half(lane, row, which):
        return factor_z.at[lane, row, pl.ds(2 * which, 2)]

    a_next, a_prev, a_far = lax.rem(a + 1, 4), lax.rem(a + 3, 4), lax.rem(a + 2, 4)
    b_next, b_prev, b_far = lax.rem(b + 1, 4), lax.rem(b + 3, 4), lax.rem(b + 2, 4)
    to_b_next, to_b_prev = device(z, a, b_next), device(z, a, b_prev)
    to_a_next, to_a_prev = device(z, a_next, b), device(z, a_prev, b)

    def along_a(row, order):
        send(piece(a, row), piece(a, row), two_sem.at[0, order], to_a_next)
        send(piece(a, row), piece(a, row), two_sem.at[1, order], to_a_prev)

    wait_bytes(piece(a, b), spread_sem)
    send(piece(a, b), piece(a, b), one_sem.at[0], to_b_next)
    send(piece(a, b), piece(a, b), one_sem.at[1], to_b_prev)
    send(piece(a, b), piece(a, b), one_sem.at[2], device(z, a, b_far))
    for copy in sent[-3:-1]:
        copy.wait_send()
    along_a(b, 0)

    wait_bytes(piece(a, b_prev), one_sem.at[0])
    along_a(b_prev, 1)
    wait_bytes(piece(a, b_next), one_sem.at[1])
    along_a(b_next, 2)
    wait_bytes(piece(a, b_far), one_sem.at[2])
    along_a(b_far, 3)
    row_order = (b, b_prev, b_next, b_far)

    def relay(order):
        row = row_order[order]
        wait_bytes(piece(a_prev, row), two_sem.at[0, order])
        send(half(a_prev, row, 0), half(a_prev, row, 0), two_sem.at[2, order], to_a_next)
        wait_bytes(piece(a_next, row), two_sem.at[1, order])
        send(half(a_next, row, 1), half(a_next, row, 1), two_sem.at[3, order], to_a_prev)

    def compute(number, lane):
        def prepare(step, carry):
            value = jnp.stack([factor_z[lane, row, step] for row in range(4)], axis=1).reshape(256, 128)
            value = value * jnp.where(step < 2, keep_low, keep_high)
            high, low = split(value)
            at = pl.ds(pl.multiple_of(step * 256, 256), 256)
            factor_split[at, 0:128] = high
            factor_split[at, 128:256] = low
            return carry

        lax.fori_loop(0, 4, prepare, 0)

        def multiply(step, carry):
            at = pl.ds(pl.multiple_of(step * 128, 128), 128)
            both = dot(tiles_hi[at, :], factor_split[...])
            result = both[:, 0:128] + both[:, 128:256] + dot(tiles_lo[at, :], factor_split[:, 0:128])
            part[number, pl.ds(lax.rem(step, 2) * 4, 4), step // 2] = result.reshape(4, 32, 128)
            return carry

        lax.fori_loop(0, 4, multiply, 0)

    to_z_next, to_z_prev = (lax.rem(z + 1, 8), p), (lax.rem(z + 7, 8), p)

    def hops(number):
        return (4, 3) if number % 2 == 0 else (3, 4)

    def ring(number, step):
        forward, backward = hops(number)
        if step < forward:
            dest = lax.rem(z + forward - step, 8)
            if step:
                wait_bytes(arrive.at[number, step - 1], ring_sem.at[number, step - 1])
                part[number, dest] = part[number, dest] + arrive[number, step - 1]
            send(part.at[number, dest], arrive.at[number, step], ring_sem.at[number, step], to_z_next)
        if step < backward:
            dest = lax.rem(z + 8 - backward + step, 8)
            slot = forward + step
            if step:
                wait_bytes(arrive.at[number, slot - 1], ring_sem.at[number, slot - 1])
                part[number, dest] = part[number, dest] + arrive[number, slot - 1]
            send(part.at[number, dest], arrive.at[number, slot], ring_sem.at[number, slot], to_z_prev)

    def publish(number, lane, value):
        rows[core, lane] = value.reshape(64, 128)
        send(rows.at[core, lane], rows.at[core, lane], rows_sem.at[number], partner)

    def ring_end(number, lane):
        forward, _ = hops(number)
        wait_bytes(arrive.at[number, forward - 1], ring_sem.at[number, forward - 1])
        wait_bytes(arrive.at[number, 6], ring_sem.at[number, 6])
        publish(number, lane, part[number, z] + arrive[number, forward - 1] + arrive[number, 6])

    def along(distance):
        return lax.rem(z + 8 + (1 - 2 * core) * distance, 8)

    def pair_send(number, slot, dest, to):
        send(
            part.at[number, along(dest)], arrive.at[number, slot], ring_sem.at[number, slot], (along(to), p)
        )

    def pairs_start(number):
        pair_send(number, 0, 4, 1)
        pair_send(number, 1, 2, 1)
        pair_send(number, 2, -3, -1)
        pair_send(number, 3, -1, -1)

    def pairs_middle(number):
        for slot, dest in ((0, 3), (2, -2), (1, 1)):
            wait_bytes(arrive.at[number, slot], ring_sem.at[number, slot])
            part[number, along(dest)] = part[number, along(dest)] + arrive[number, slot]
            pair_send(number, slot + 4, dest, dest)

    def pairs_end(number, lane):
        value = part[number, z]
        for slot in range(3, 7):
            wait_bytes(arrive.at[number, slot], ring_sem.at[number, slot])
            value = value + arrive[number, slot]
        publish(number, lane, value)

    compute(0, a)
    pairs_start(0)
    relay(0)
    relay(1)
    relay(2)
    pairs_middle(0)
    relay(3)
    compute(1, a_prev)
    pairs_start(1)
    compute(2, a_next)
    pairs_start(2)
    pairs_end(0, a)
    for order in range(4):
        wait_bytes(half(a_far, row_order[order], 0), two_sem.at[2, order])
        wait_bytes(half(a_far, row_order[order], 1), two_sem.at[3, order])
    compute(3, a_far)
    pairs_start(3)
    pairs_middle(1)
    pairs_middle(2)
    pairs_middle(3)
    pairs_end(1, a_prev)
    pairs_end(2, a_next)
    pairs_end(3, a_far)
    for number in range(CHUNKS):
        wait_bytes(rows.at[1 - core, 0], rows_sem.at[number])

    def joined(number):
        return jnp.concatenate([rows[number, lane] for lane in range(4)], axis=1)

    off0 = joined(0) * (-keep0)
    total[0] = off0
    total[3] = masked1
    put_left(192, off0)
    put_right(0, total[0, :, half_cols])
    put_right(192, total[3, :, half_cols])

    flip = (((0,), (0,)), ((), ()))

    def product(mat, first_row, row_count, right_row, swap):
        def go(step, carry):
            lanes = pl.ds(pl.multiple_of(step * 128, 128), 128)
            value = lax.dot_general(
                left_buf[first_row:first_row + row_count, lanes],
                right_buf[right_row:right_row + row_count, :],
                flip, preferred_element_type=F32,
            )
            for inner in range(4):
                upper = step + swap * (inner - step)
                lower = inner + swap * (step - inner)
                gram[mat, upper, lower] = value[inner * 32:(inner + 1) * 32, :]
            return carry

        lax.fori_loop(0, 4, go, 0)

    own_first = (a, b, a)
    own_second = (b, a, b)
    next_first = (to_a_next, to_b_next, to_a_next)
    prev_first = (to_a_prev, to_b_prev, to_a_prev)

    def gram_start(mat):
        up = lax.rem(own_first[mat] + 1, 4)
        down = lax.rem(own_first[mat] + 3, 4)
        far = lax.rem(own_first[mat] + 2, 4)
        low, high = pl.ds(0, 2), pl.ds(2, 2)
        send(gram.at[mat, far, low], gram_in.at[mat, 0], gram_sem.at[mat, 0], next_first[mat])
        send(gram.at[mat, far, high], gram_in.at[mat, 1], gram_sem.at[mat, 1], prev_first[mat])
        send(gram.at[mat, up, high], gram_in.at[mat, 2], gram_sem.at[mat, 2], next_first[mat])
        send(gram.at[mat, down, low], gram_in.at[mat, 3], gram_sem.at[mat, 3], prev_first[mat])

    def gram_middle(mat):
        up = lax.rem(own_first[mat] + 1, 4)
        down = lax.rem(own_first[mat] + 3, 4)
        low, high = pl.ds(0, 2), pl.ds(2, 2)
        wait_bytes(gram_in.at[mat, 0], gram_sem.at[mat, 0])
        gram[mat, up, low] = gram[mat, up, low] + gram_in[mat, 0]
        send(gram.at[mat, up, low], gram_in.at[mat, 4], gram_sem.at[mat, 4], next_first[mat])
        wait_bytes(gram_in.at[mat, 1], gram_sem.at[mat, 1])
        gram[mat, down, high] = gram[mat, down, high] + gram_in[mat, 1]
        send(gram.at[mat, down, high], gram_in.at[mat, 5], gram_sem.at[mat, 5], prev_first[mat])

    def gram_end(mat):
        here = own_first[mat]
        low, high = pl.ds(0, 2), pl.ds(2, 2)
        wait_bytes(gram_in.at[mat, 2], gram_sem.at[mat, 2])
        wait_bytes(gram_in.at[mat, 3], gram_sem.at[mat, 3])
        wait_bytes(gram_in.at[mat, 4], gram_sem.at[mat, 4])
        wait_bytes(gram_in.at[mat, 5], gram_sem.at[mat, 5])
        line[mat, low] = gram[mat, here, low] + gram_in[mat, 3] + gram_in[mat, 4]
        line[mat, high] = gram[mat, here, high] + gram_in[mat, 2] + gram_in[mat, 5]
        for step in range(1, 4):
            other = lax.rem(own_second[mat] + step, 4)
            target = device(z, a, other) if mat != 1 else device(z, other, b)
            send(line.at[mat, other], line_in.at[mat, step - 1], line_sem.at[mat, step - 1], target)

    def line_end(mat):
        for step in range(3):
            wait_bytes(line_in.at[mat, step], line_sem.at[mat, step])
        value = line[mat, own_second[mat]] + line_in[mat, 0] + line_in[mat, 1] + line_in[mat, 2]
        for row in range(4):
            for lane in range(2):
                plane[2 * row + lane, mat] = value[row * 8:(row + 1) * 8, lane * 128:(lane + 1) * 128]

    product(0, 0, 192, 0, core)
    gram_start(0)
    product(1, 192, 192, 192, 1 - core)
    gram_start(1)

    shifted = dot3(split(off0), link_pair)
    total[1] = shifted
    put_left(576, shifted)
    inner = joined(1) + shifted
    total[2] = inner
    put_right(384, total[2, :, half_cols])
    put_right(576, total[3, :, half_cols])
    put_right(768, total[1, :, half_cols])
    product(2, 384, 576, 384, core)
    gram_start(2)

    mine_rows = pl.ds(pl.multiple_of(core * 32, 32), 32)
    off_ref[0] = total[0, mine_rows, :]
    off_ref[1] = total[2, mine_rows, :] * (-keep1)

    for mat in range(3):
        gram_middle(mat)
    for mat in range(3):
        gram_end(mat)
    for mat in range(3):
        line_end(mat)

    for step in RING8:
        dest_z = lax.rem(z + step, 8)
        send_group(plane.at[dest_z], z_in.at[z], z_sem, (dest_z, p), 2)
    local(plane.at[z], z_in.at[z], z_sem)
    wait_bytes(z_in, z_sem)
    value = z_in[0]
    for other in range(1, 8):
        value = value + z_in[other]
    plane_total = final.at[8]
    final[8] = value
    owner = z // 4
    slot = lax.rem(z, 4) * 2 + core
    for step in RING8:
        send_group(plane_total, final.at[slot], final_sem, (lax.rem(z + step, 8), (p // 2) * 2 + owner), 3)

    @pl.when(owner == core)
    def _():
        local(plane_total, final.at[slot], final_sem)

    @pl.when(owner != core)
    def _():
        send_group(plane_total, final.at[slot], final_sem, partner, 4)

    wait_bytes(final.at[pl.ds(0, 8)], final_sem)

    def slice_of(mat):
        tiles = []
        for row in range(2):
            lanes = [final[(2 * row + lane) * 2 + side, mat] for side in range(2) for lane in range(2)]
            tiles.append(jnp.concatenate(lanes, axis=1))
        return jnp.concatenate(tiles, axis=0)

    diag0 = dinv1_v[0] + slice_of(0)
    diag_ref[0] = diag0
    link_ref[0] = -(slice_of(1) + dot3(split(diag0), (link_hi[...], link_lo[...])))
    diag_ref[1] = dinv1_v[1] + extra[...] + slice_of(2)

    for number, copy in enumerate(sent):
        if number not in (2, 3):
            copy.wait_send()
    wait_bytes(first.at[pl.ds(0, 31)], group_send.at[0])
    wait_bytes(first.at[pl.ds(0, 28)], group_send.at[1])
    wait_bytes(plane.at[pl.ds(0, 7)], group_send.at[2])
    wait_bytes(plane.at[pl.ds(0, 7)], group_send.at[3])

    @pl.when(owner != core)
    def _():
        wait_bytes(plane.at[0], group_send.at[4])


def body(inverse_tiles, factor, link_factor, diag_inverse, ancestors):
    anywhere = pl.BlockSpec(memory_space=pltpu.MemorySpace.HBM)
    vmem = pl.BlockSpec(memory_space=pltpu.VMEM)
    dma = pltpu.SemaphoreType.DMA
    return pl.pallas_call(
        kernel,
        out_shape=(
            jax.ShapeDtypeStruct((2, 32, 512), F32),
            jax.ShapeDtypeStruct((2, 16, 512), F32),
            jax.ShapeDtypeStruct((1, 16, 512), F32),
        ),
        in_specs=[anywhere] * 5,
        out_specs=(vmem, vmem, vmem),
        scratch_shapes=[
            pltpu.SMEM((2, 8), jnp.int32),
            pltpu.VMEM((2, 256, 1024), F32),
            pltpu.VMEM((512, 1024), BF16),
            pltpu.VMEM((512, 1024), BF16),
            pltpu.VMEM((32, 8, 128), F32),
            pltpu.VMEM((4, 4, 4, 8, 8, 128), F32),
            pltpu.VMEM((1024, 256), BF16),
            pltpu.VMEM((CHUNKS, 8, 2, 32, 128), F32),
            pltpu.VMEM((CHUNKS, 7, 2, 32, 128), F32),
            pltpu.VMEM((2, 4, 64, 128), F32),
            pltpu.VMEM((2, 2, 32, 512), F32),
            pltpu.VMEM((512, 512), F32),
            pltpu.VMEM((512, 512), BF16),
            pltpu.VMEM((512, 512), BF16),
            pltpu.VMEM((512, 512), F32),
            pltpu.VMEM((2, 16, 512), F32),
            pltpu.VMEM((16, 512), F32),
            pltpu.VMEM((960, 512), BF16),
            pltpu.VMEM((960, 256), BF16),
            pltpu.VMEM((3, 4, 4, 32, 256), F32),
            pltpu.VMEM((3, 6, 2, 32, 256), F32),
            pltpu.VMEM((3, 4, 32, 256), F32),
            pltpu.VMEM((3, 3, 32, 256), F32),
            pltpu.VMEM((8, 3, 8, 128), F32),
            pltpu.VMEM((8, 3, 8, 128), F32),
            pltpu.VMEM((4, 64, 512), F32),
            pltpu.VMEM((9, 3, 8, 128), F32),
            dma((6,)),
            dma,
            dma,
            dma((2,)),
            dma((4,)),
            dma((4, 4)),
            dma((CHUNKS, 7)),
            dma((CHUNKS,)),
            dma((3, 6)),
            dma((3, 3)),
            dma,
            dma,
            dma((96,)),
            dma((5,)),
        ],
        compiler_params=pltpu.CompilerParams(
            collective_id=0, has_side_effects=True, vmem_limit_bytes=67043328
        ),
    )(inverse_tiles, factor, link_factor, diag_inverse, ancestors)


def solution(mesh):
    in_specs = (P("pcol", "prow"), P(None, ("pcol", "prow"), None), P(), P(), P())
    out_specs = (P(None, ("pcol", "prow"), None), P(None, "pcol", None), P(None, "pcol", None))
    return jax.shard_map(body, mesh=mesh, in_specs=in_specs, out_specs=out_specs, check_vma=False)
```

```python
import functools

import jax
import jax.numpy as jnp
from jax import lax
from jax.experimental import pallas as pl
from jax.experimental.pallas import tpu as pltpu
from jax.sharding import PartitionSpec as P

MESH = pl.DeviceIdType.MESH
F32 = jnp.float32
BF16 = jnp.bfloat16
CHUNKS = 4
RING8 = (4, 3, 5, 2, 6, 1, 7)
PLANE = sorted(
    ((dx, dy, dc) for dx in range(4) for dy in range(4) for dc in range(2) if dx or dy or dc),
    key=lambda at: -(min(at[0], 4 - at[0]) + min(at[1], 4 - at[1]) + 0.5 * at[2]),
)


def split(value):
    high = value.astype(BF16)
    low = (value - high.astype(F32)).astype(BF16)
    return high, low


def dot(left, right):
    return jnp.dot(left, right, preferred_element_type=F32)


def dot3(left, right):
    left_high, left_low = left
    right_high, right_low = right
    return dot(left_high, right_high) + dot(left_high, right_low) + dot(left_low, right_high)


def kernel(
    tiles_hbm, factor_hbm, link_hbm, dinv_hbm, anc_hbm,
    out_ref,
    anc_ref, tiles_v, tiles_hi, tiles_lo, first, factor_z, factor_split, part, arrive, rows, pair_factor,
    link_v, link_hi, link_lo, dinv0_v, dinv1_v, extra,
    left_buf, right_buf, gram, gram_in, line, line_in, plane, z_in, total, final,
    local_sem, first_sem, spread_sem, pair_sem, one_sem, two_sem, far_sem, ring_sem, rows_sem,
    gram_sem, line_sem, z_sem, final_sem, group_send,
):
    z = lax.axis_index("prow")
    p = lax.axis_index("pcol")
    core = lax.rem(p, 2)
    x = p // 8
    y = lax.rem(p // 2, 4)
    a = x + core * (y - x)
    b = y + core * (x - y)
    block = p // 2

    def device(dest_z, dest_a, dest_b):
        dest_x = dest_a + core * (dest_b - dest_a)
        dest_y = dest_b + core * (dest_a - dest_b)
        return (dest_z, (dest_x * 4 + dest_y) * 2 + core)

    def local(src, dst, sem):
        copy = pltpu.make_async_copy(src, dst, sem)
        copy.start()
        return copy

    def send(src, dst, recv, target, group):
        pltpu.make_async_remote_copy(
            src_ref=src, dst_ref=dst, send_sem=group_send.at[group], recv_sem=recv,
            device_id=target, device_id_type=MESH,
        ).start()

    def wait_bytes(ref, sem):
        pltpu.make_async_copy(ref, ref, sem).wait()

    own_pair = local(factor_hbm, pair_factor.at[core], local_sem.at[4])
    own_anc = local(anc_hbm, anc_ref, local_sem.at[5])
    own_tiles = local(tiles_hbm, tiles_v.at[core], local_sem.at[0])
    own_link = local(link_hbm.at[0], link_v, local_sem.at[1])
    own_dinv0 = local(dinv_hbm.at[0], dinv0_v, local_sem.at[2])
    slice_rows = pl.ds(pl.multiple_of(p * 16, 16), 16)
    own_dinv1 = local(dinv_hbm.at[:, slice_rows], dinv1_v, local_sem.at[3])

    barrier = pltpu.get_barrier_semaphore()
    def in_plane(offset):
        dx, dy, dc = offset
        return lax.rem(x + dx, 4) * 8 + lax.rem(y + dy, 4) * 2 + (1 - core if dc else core)

    for offset in PLANE:
        pl.semaphore_signal(barrier, inc=1, device_id=(z, in_plane(offset)), device_id_type=MESH)
    for step in RING8:
        for other in range(2):
            pl.semaphore_signal(
                barrier, inc=1, device_id=(lax.rem(z + step, 8), (p // 2) * 2 + other), device_id_type=MESH
            )
    pl.semaphore_wait(barrier, 31 + 14)

    partner = (z, p + 1 - 2 * core)

    def tile_of(target):
        number = lax.rem(target, 2)
        tx = target // 8
        ty = lax.rem(target // 2, 4)
        lane = tx + number * (ty - tx)
        row = ty + number * (tx - ty)
        return pair_factor.at[
            core, number, pl.ds(pl.multiple_of(row * 8, 8), 8), pl.ds(pl.multiple_of(lane * 128, 128), 128)
        ]

    own_pair.wait()
    for offset in PLANE:
        target = in_plane(offset)
        send(tile_of(target), first.at[p], first_sem, (z, target), 0)
    local(tile_of(p), first.at[p], first_sem)

    send(tiles_hbm, tiles_v.at[core], pair_sem.at[0], partner, 5)
    send(pair_factor.at[core], pair_factor.at[core], pair_sem.at[1], partner, 6)

    def keep_of(number, row_block):
        listed = anc_ref[number, 0] == row_block
        for entry in range(1, anc_ref.shape[1]):
            listed = jnp.logical_or(listed, anc_ref[number, entry] == row_block)
        return jnp.where(listed, jnp.float32(1), jnp.float32(0))

    own_anc.wait()
    keep_low = keep_of(core, 2 * z)
    keep_high = keep_of(core, 2 * z + 1)
    keep0 = keep_of(0, block)
    keep1 = keep_of(1, block)

    own_tiles.wait()

    def split_tiles(half):
        def go(step, carry):
            at = pl.ds(pl.multiple_of(step * 32, 32), 32)
            high, low = split(tiles_v[half, at, :])
            put = pl.ds(pl.multiple_of(half * 256 + step * 32, 32), 32)
            tiles_hi[put, :] = high
            tiles_lo[put, :] = low
            return carry

        lax.fori_loop(0, 8, go, 0)

    split_tiles(core)
    own_link.wait()
    own_dinv0.wait()
    own_dinv1.wait()

    def split_link(step, carry):
        at = pl.ds(pl.multiple_of(step * 32, 32), 32)
        high, low = split(link_v[at, :])
        link_hi[at, :] = high
        link_lo[at, :] = low
        return carry

    lax.fori_loop(0, 16, split_link, 0)

    row_ids = lax.broadcasted_iota(jnp.int32, (16, 512), 0) + p * 16
    col_ids = lax.broadcasted_iota(jnp.int32, (16, 512), 1)
    pick = jnp.where(row_ids == col_ids, jnp.float32(1), jnp.float32(0)).astype(BF16)
    across = (((1,), (1,)), ((), ()))
    picked = lax.dot_general(pick, link_hi[...], across, preferred_element_type=F32) + lax.dot_general(
        pick, link_lo[...], across, preferred_element_type=F32
    )
    picked = dot3(split(picked), split(dinv0_v[...]))
    extra[0] = dot3(split(picked), (link_hi[...], link_lo[...]))
    extra[1] = dot3(split(dinv1_v[0]), (link_hi[...], link_lo[...]))

    wait_bytes(first, first_sem)
    mine = factor_z.at[a, b, :, z]
    for step in RING8:
        dest_z = lax.rem(z + step, 8)
        send(first.at[pl.ds(4 * dest_z, 4)], mine, spread_sem, (dest_z, p), 1)
    local(first.at[pl.ds(4 * z, 4)], mine, spread_sem)

    wait_bytes(tiles_v.at[1 - core], pair_sem.at[0])
    split_tiles(1 - core)

    wait_bytes(pair_factor.at[1 - core], pair_sem.at[1])

    def own_rows(number, keep):
        return jnp.concatenate([pair_factor[0, number], pair_factor[1, number]], axis=0) * keep

    masked0 = own_rows(0, keep0)
    masked1 = own_rows(1, keep1)
    link_pair = (link_hi[...], link_lo[...])
    linked0 = dot3(split(masked0), link_pair)

    def put(buffer, segment, terms):
        for number, term in enumerate(terms):
            at = segment * 192 + number * 64
            buffer[at:at + 64, :] = term

    def put_left(segment, value):
        high, low = split(value)
        put(left_buf, segment, (high, high, low))

    half_cols = pl.ds(pl.multiple_of(core * 256, 256), 256)

    def put_right(segments, number):
        high, low = split(total[number, :, half_cols])
        for segment in segments:
            put(right_buf, segment, (high, low, high))

    total[3] = masked1
    put_left(0, -masked0)
    put_left(2, masked1)
    put_left(4, -linked0)
    put_right((2, 4), 3)

    def piece(lane, row):
        return factor_z.at[lane, row]

    def half(lane, row, which):
        return factor_z.at[lane, row, pl.ds(2 * which, 2)]

    a_next, a_prev, a_far = lax.rem(a + 1, 4), lax.rem(a + 3, 4), lax.rem(a + 2, 4)
    b_next, b_prev, b_far = lax.rem(b + 1, 4), lax.rem(b + 3, 4), lax.rem(b + 2, 4)
    to_b_next, to_b_prev = device(z, a, b_next), device(z, a, b_prev)
    to_a_next, to_a_prev = device(z, a_next, b), device(z, a_prev, b)

    def along_a(row, order):
        send(piece(a, row), piece(a, row), two_sem.at[0, order], to_a_next, 8)
        send(piece(a, row), piece(a, row), two_sem.at[1, order], to_a_prev, 8)

    wait_bytes(piece(a, b), spread_sem)
    send(piece(a, b), piece(a, b), one_sem.at[0], to_b_next, 7)
    send(piece(a, b), piece(a, b), one_sem.at[1], to_b_prev, 7)
    send(piece(a, b), piece(a, b), one_sem.at[2], device(z, a, b_far), 13)
    along_a(b, 0)
    row_order = (b, b_prev, b_next, b_far)

    def relay(order):
        row = row_order[order]
        wait_bytes(piece(a_prev, row), two_sem.at[0, order])
        send(half(a_prev, row, 0), half(a_prev, row, 0), far_sem, to_a_next, 8)
        wait_bytes(piece(a_next, row), two_sem.at[1, order])
        send(half(a_next, row, 1), half(a_next, row, 1), far_sem, to_a_prev, 8)

    wait_bytes(piece(a, b_prev), one_sem.at[0])
    along_a(b_prev, 1)
    wait_bytes(piece(a, b_next), one_sem.at[1])
    along_a(b_next, 2)
    relay(0)
    wait_bytes(piece(a, b_far), one_sem.at[2])
    along_a(b_far, 3)
    send(piece(a, b_far), piece(a, b_far), far_sem, device(z, a_far, b), 8)
    relay(1)

    def compute(number, lane):
        def prepare(step, carry):
            value = jnp.stack([factor_z[lane, row, step] for row in range(4)], axis=1).reshape(256, 128)
            value = value * jnp.where(step < 2, keep_low, keep_high)
            high, low = split(value)
            at = pl.ds(pl.multiple_of(step * 256, 256), 256)
            factor_split[at, 0:128] = high
            factor_split[at, 128:256] = low
            return carry

        lax.fori_loop(0, 4, prepare, 0)

        def multiply(step, carry):
            at = pl.ds(pl.multiple_of(step * 256, 256), 256)
            both = dot(tiles_hi[at, :], factor_split[...])
            result = both[:, 0:128] + both[:, 128:256] + dot(tiles_lo[at, :], factor_split[:, 0:128])
            part[number, :, step] = result.reshape(8, 32, 128)
            return carry

        lax.fori_loop(0, 2, multiply, 0)

    def publish(number, lane, value):
        rows[core, lane] = value.reshape(64, 128)
        send(rows.at[core, lane], rows.at[core, lane], rows_sem, partner, 10)

    def along(distance):
        return lax.rem(z + 8 + (1 - 2 * core) * distance, 8)

    def pair_send(number, slot, dest, to):
        send(
            part.at[number, along(dest)], arrive.at[number, slot], ring_sem.at[number, min(slot, 3)], (along(to), p), 9
        )

    def pairs_start(number):
        pair_send(number, 0, 4, 1)
        pair_send(number, 1, 2, 1)
        pair_send(number, 2, -3, -1)
        pair_send(number, 3, -1, -1)

    def pairs_middle(number):
        for slot, dest in ((0, 3), (2, -2), (1, 1)):
            wait_bytes(arrive.at[number, slot], ring_sem.at[number, slot])
            part[number, along(dest)] = part[number, along(dest)] + arrive[number, slot]
            pair_send(number, slot + 4, dest, dest)

    def pairs_end(number, lane):
        wait_bytes(arrive.at[number, pl.ds(3, 4)], ring_sem.at[number, 3])
        value = part[number, z]
        for slot in range(3, 7):
            value = value + arrive[number, slot]
        publish(number, lane, value)

    compute(0, a)
    pairs_start(0)
    relay(2)
    pairs_middle(0)
    wait_bytes(piece(a_prev, b_far), two_sem.at[0, 3])
    wait_bytes(piece(a_next, b_far), two_sem.at[1, 3])
    compute(1, a_prev)
    pairs_start(1)
    compute(2, a_next)
    pairs_start(2)
    pairs_end(0, a)
    wait_bytes(factor_z.at[a_far], far_sem)
    compute(3, a_far)
    pairs_start(3)
    pairs_middle(1)
    pairs_middle(2)
    pairs_middle(3)
    pairs_end(1, a_prev)
    pairs_end(2, a_next)
    pairs_end(3, a_far)
    wait_bytes(rows.at[1 - core], rows_sem)

    def joined(number):
        return jnp.concatenate([rows[number, lane] for lane in range(4)], axis=1)

    flip = (((0,), (0,)), ((), ()))

    def product(mat, left_segment, right_segment, segments, swap):
        def go(step, carry):
            lanes = pl.ds(pl.multiple_of(step * 128, 128), 128)
            value = lax.dot_general(
                left_buf[left_segment * 192:(left_segment + segments) * 192, lanes],
                right_buf[right_segment * 192:(right_segment + segments) * 192, :],
                flip, preferred_element_type=F32,
            )
            for inner in range(4):
                upper = step + swap * (inner - step)
                lower = inner + swap * (step - inner)
                gram[mat, upper, lower] = value[inner * 32:(inner + 1) * 32, :]
            return carry

        lax.fori_loop(0, 4, go, 0)

    own_first = (a, b, a)
    own_second = (b, a, b)
    next_first = (to_a_next, to_b_next, to_a_next)
    prev_first = (to_a_prev, to_b_prev, to_a_prev)

    def gram_start(mat):
        up = lax.rem(own_first[mat] + 1, 4)
        down = lax.rem(own_first[mat] + 3, 4)
        far = lax.rem(own_first[mat] + 2, 4)
        low, high = pl.ds(0, 2), pl.ds(2, 2)
        send(gram.at[mat, far, low], gram_in.at[mat, 0], gram_sem.at[mat, 0], next_first[mat], 11)
        send(gram.at[mat, far, high], gram_in.at[mat, 1], gram_sem.at[mat, 1], prev_first[mat], 11)
        send(gram.at[mat, up, high], gram_in.at[mat, 2], gram_sem.at[mat, 2], next_first[mat], 11)
        send(gram.at[mat, down, low], gram_in.at[mat, 3], gram_sem.at[mat, 2], prev_first[mat], 11)

    def gram_middle(mat):
        up = lax.rem(own_first[mat] + 1, 4)
        down = lax.rem(own_first[mat] + 3, 4)
        low, high = pl.ds(0, 2), pl.ds(2, 2)
        wait_bytes(gram_in.at[mat, 0], gram_sem.at[mat, 0])
        gram[mat, up, low] = gram[mat, up, low] + gram_in[mat, 0]
        send(gram.at[mat, up, low], gram_in.at[mat, 4], gram_sem.at[mat, 2], next_first[mat], 11)
        wait_bytes(gram_in.at[mat, 1], gram_sem.at[mat, 1])
        gram[mat, down, high] = gram[mat, down, high] + gram_in[mat, 1]
        send(gram.at[mat, down, high], gram_in.at[mat, 5], gram_sem.at[mat, 2], prev_first[mat], 11)

    def gram_end(mat):
        here = own_first[mat]
        low, high = pl.ds(0, 2), pl.ds(2, 2)
        wait_bytes(gram_in.at[mat, pl.ds(2, 4)], gram_sem.at[mat, 2])
        line[mat, low] = gram[mat, here, low] + gram_in[mat, 3] + gram_in[mat, 4]
        line[mat, high] = gram[mat, here, high] + gram_in[mat, 2] + gram_in[mat, 5]
        for step in range(1, 4):
            other = lax.rem(own_second[mat] + step, 4)
            target = device(z, a, other) if mat != 1 else device(z, other, b)
            send(line.at[mat, other], line_in.at[mat, step - 1], line_sem.at[mat], target, 12)

    def line_end(mat):
        wait_bytes(line_in.at[mat], line_sem.at[mat])
        value = line[mat, own_second[mat]] + line_in[mat, 0] + line_in[mat, 1] + line_in[mat, 2]
        for row in range(4):
            for lane in range(2):
                plane[2 * row + lane, mat] = value[row * 8:(row + 1) * 8, lane * 128:(lane + 1) * 128]

    off0 = joined(0) * (-keep0)
    total[0] = off0
    put_right((0,), 0)
    product(0, 0, 0, 1, core)
    gram_start(0)

    put_left(1, off0)
    shifted = dot3(split(off0), link_pair)
    total[1] = shifted
    put_right((1, 5), 1)
    product(1, 0, 1, 2, 1 - core)
    gram_start(1)

    put_left(3, shifted)
    total[2] = joined(1) + shifted
    put_right((3,), 2)
    product(2, 2, 3, 3, core)
    gram_start(2)

    mine_rows = pl.ds(pl.multiple_of(core * 32, 32), 32)
    out_ref[0:32] = total[0, mine_rows, :]
    out_ref[32:64] = total[2, mine_rows, :] * (-keep1)

    for mat in range(3):
        gram_middle(mat)
    for mat in range(3):
        gram_end(mat)
    for mat in range(3):
        line_end(mat)

    for step in RING8:
        dest_z = lax.rem(z + step, 8)
        send(plane.at[dest_z], z_in.at[z], z_sem, (dest_z, p), 2)
    local(plane.at[z], z_in.at[z], z_sem)
    wait_bytes(z_in, z_sem)
    value = z_in[0]
    for other in range(1, 8):
        value = value + z_in[other]
    plane_total = final.at[8]
    final[8] = value
    owner = z // 4
    slot = lax.rem(z, 4) * 2 + core
    for step in RING8:
        send(plane_total, final.at[slot], final_sem, (lax.rem(z + step, 8), (p // 2) * 2 + owner), 3)

    @pl.when(owner == core)
    def _():
        local(plane_total, final.at[slot], final_sem)

    @pl.when(owner != core)
    def _():
        send(plane_total, final.at[slot], final_sem, partner, 4)

    wait_bytes(final.at[pl.ds(0, 8)], final_sem)

    def slice_of(mat):
        tiles = []
        for row in range(2):
            lanes = [final[(2 * row + lane) * 2 + side, mat] for side in range(2) for lane in range(2)]
            tiles.append(jnp.concatenate(lanes, axis=1))
        return jnp.concatenate(tiles, axis=0)

    out_ref[64:80] = dinv1_v[0] + slice_of(0)
    out_ref[80:96] = dinv1_v[1] + extra[0] + slice_of(2)
    out_ref[96:112] = -(extra[1] + slice_of(1))

    wait_bytes(factor_z.at[0, pl.ds(0, 2)], group_send.at[7])
    wait_bytes(tiles_v.at[0], group_send.at[5])
    wait_bytes(pair_factor.at[0], group_send.at[6])
    wait_bytes(factor_z.at[pl.ds(0, 3)], group_send.at[8])
    wait_bytes(arrive, group_send.at[9])
    wait_bytes(rows.at[0], group_send.at[10])
    wait_bytes(gram_in, group_send.at[11])
    wait_bytes(line_in, group_send.at[12])
    wait_bytes(factor_z.at[0, 0], group_send.at[13])
    wait_bytes(first.at[pl.ds(0, 31)], group_send.at[0])
    wait_bytes(first.at[pl.ds(0, 28)], group_send.at[1])
    wait_bytes(plane.at[pl.ds(0, 7)], group_send.at[2])
    wait_bytes(plane.at[pl.ds(0, 7)], group_send.at[3])

    @pl.when(owner != core)
    def _():
        wait_bytes(plane.at[0], group_send.at[4])


def part_out(all_ref, off_ref, diag_ref, link_ref):
    off_ref[...] = all_ref[0:64].reshape(2, 32, 512)
    diag_ref[...] = all_ref[64:96].reshape(2, 16, 512)
    link_ref[...] = all_ref[96:112].reshape(1, 16, 512)


def body(inverse_tiles, factor, link_factor, diag_inverse, ancestors):
    anywhere = pl.BlockSpec(memory_space=pltpu.MemorySpace.HBM)
    vmem = pl.BlockSpec(memory_space=pltpu.VMEM)
    dma = pltpu.SemaphoreType.DMA
    out = pl.pallas_call(
        kernel,
        out_shape=jax.ShapeDtypeStruct((112, 512), F32),
        in_specs=[anywhere] * 5,
        out_specs=vmem,
        scratch_shapes=[
            pltpu.SMEM((2, 8), jnp.int32),
            pltpu.VMEM((2, 256, 1024), F32),
            pltpu.VMEM((512, 1024), BF16),
            pltpu.VMEM((512, 1024), BF16),
            pltpu.VMEM((32, 8, 128), F32),
            pltpu.VMEM((4, 4, 4, 8, 8, 128), F32),
            pltpu.VMEM((1024, 256), BF16),
            pltpu.VMEM((CHUNKS, 8, 2, 32, 128), F32),
            pltpu.VMEM((CHUNKS, 7, 2, 32, 128), F32),
            pltpu.VMEM((2, 4, 64, 128), F32),
            pltpu.VMEM((2, 2, 32, 512), F32),
            pltpu.VMEM((512, 512), F32),
            pltpu.VMEM((512, 512), BF16),
            pltpu.VMEM((512, 512), BF16),
            pltpu.VMEM((512, 512), F32),
            pltpu.VMEM((2, 16, 512), F32),
            pltpu.VMEM((2, 16, 512), F32),
            pltpu.VMEM((960, 512), BF16),
            pltpu.VMEM((1152, 256), BF16),
            pltpu.VMEM((3, 4, 4, 32, 256), F32),
            pltpu.VMEM((3, 6, 2, 32, 256), F32),
            pltpu.VMEM((3, 4, 32, 256), F32),
            pltpu.VMEM((3, 3, 32, 256), F32),
            pltpu.VMEM((8, 3, 8, 128), F32),
            pltpu.VMEM((8, 3, 8, 128), F32),
            pltpu.VMEM((4, 64, 512), F32),
            pltpu.VMEM((9, 3, 8, 128), F32),
            dma((6,)),
            dma,
            dma,
            dma((2,)),
            dma((3,)),
            dma((2, 4)),
            dma,
            dma((CHUNKS, 4)),
            dma,
            dma((3, 3)),
            dma((3,)),
            dma,
            dma,
            dma((14,)),
        ],
        compiler_params=pltpu.CompilerParams(
            collective_id=0, has_side_effects=True, vmem_limit_bytes=67043328
        ),
    )(inverse_tiles, factor, link_factor, diag_inverse, ancestors)
    return pl.pallas_call(
        part_out,
        out_shape=(
            jax.ShapeDtypeStruct((2, 32, 512), F32),
            jax.ShapeDtypeStruct((2, 16, 512), F32),
            jax.ShapeDtypeStruct((1, 16, 512), F32),
        ),
        in_specs=[vmem],
        out_specs=(vmem, vmem, vmem),
    )(out)


def solution(mesh):
    in_specs = (P("pcol", "prow"), P(None, ("pcol", "prow"), None), P(), P(), P())
    out_specs = (P(None, ("pcol", "prow"), None), P(None, "pcol", None), P(None, "pcol", None))
    return jax.shard_map(body, mesh=mesh, in_specs=in_specs, out_specs=out_specs, check_vma=False)
```

```python
import functools

import jax
import jax.numpy as jnp
from jax import lax
from jax.experimental import pallas as pl
from jax.experimental.pallas import tpu as pltpu
from jax.sharding import PartitionSpec as P

MESH = pl.DeviceIdType.MESH
F32 = jnp.float32
BF16 = jnp.bfloat16
CHUNKS = 4
RING8 = (4, 3, 5, 2, 6, 1, 7)
PLANE = sorted(
    ((dx, dy, dc) for dx in range(4) for dy in range(4) for dc in range(2) if dx or dy or dc),
    key=lambda at: -(min(at[0], 4 - at[0]) + min(at[1], 4 - at[1]) + 0.5 * at[2]),
)


def split(value):
    high = value.astype(BF16)
    low = (value - high.astype(F32)).astype(BF16)
    return high, low


def dot(left, right):
    return jnp.dot(left, right, preferred_element_type=F32)


def dot3(left, right):
    left_high, left_low = left
    right_high, right_low = right
    return dot(left_high, right_high) + dot(left_high, right_low) + dot(left_low, right_high)


def kernel(
    tiles_hbm, factor_hbm, link_hbm, dinv_hbm, anc_hbm,
    out_ref,
    anc_ref, tiles_v, tiles_hi, tiles_lo, first, factor_z, factor_split, part, arrive, rows, pair_factor,
    link_v, link_hi, link_lo, dinv0_v, dinv1_v, extra,
    left_buf, right_buf, gram, gram_in, line, line_in, plane, z_in, total, final,
    local_sem, first_sem, spread_sem, pair_sem, one_sem, two_sem, far_sem, ring_sem, rows_sem,
    gram_sem, line_sem, z_sem, final_sem, group_send,
):
    z = lax.axis_index("prow")
    p = lax.axis_index("pcol")
    core = lax.rem(p, 2)
    x = p // 8
    y = lax.rem(p // 2, 4)
    a = x + core * (y - x)
    b = y + core * (x - y)
    block = p // 2

    def device(dest_z, dest_a, dest_b):
        dest_x = dest_a + core * (dest_b - dest_a)
        dest_y = dest_b + core * (dest_a - dest_b)
        return (dest_z, (dest_x * 4 + dest_y) * 2 + core)

    def local(src, dst, sem):
        copy = pltpu.make_async_copy(src, dst, sem)
        copy.start()
        return copy

    def send(src, dst, recv, target, group):
        pltpu.make_async_remote_copy(
            src_ref=src, dst_ref=dst, send_sem=group_send.at[group], recv_sem=recv,
            device_id=target, device_id_type=MESH,
        ).start()

    def wait_bytes(ref, sem):
        pltpu.make_async_copy(ref, ref, sem).wait()

    own_pair = local(factor_hbm, pair_factor.at[core], local_sem.at[4])
    own_anc = local(anc_hbm, anc_ref, local_sem.at[5])
    own_tiles = local(tiles_hbm, tiles_v.at[core], local_sem.at[0])
    own_link = local(link_hbm.at[0], link_v, local_sem.at[1])
    own_dinv0 = local(dinv_hbm.at[0], dinv0_v, local_sem.at[2])
    slice_rows = pl.ds(pl.multiple_of(p * 16, 16), 16)
    own_dinv1 = local(dinv_hbm.at[:, slice_rows], dinv1_v, local_sem.at[3])

    barrier = pltpu.get_barrier_semaphore()
    def in_plane(offset):
        dx, dy, dc = offset
        return lax.rem(x + dx, 4) * 8 + lax.rem(y + dy, 4) * 2 + (1 - core if dc else core)

    for offset in PLANE:
        pl.semaphore_signal(barrier, inc=1, device_id=(z, in_plane(offset)), device_id_type=MESH)
    for step in RING8:
        pl.semaphore_signal(barrier, inc=1, device_id=(lax.rem(z + step, 8), p), device_id_type=MESH)
    pl.semaphore_wait(barrier, 31 + 7)

    partner = (z, p + 1 - 2 * core)

    def tile_of(target):
        number = lax.rem(target, 2)
        tx = target // 8
        ty = lax.rem(target // 2, 4)
        lane = tx + number * (ty - tx)
        row = ty + number * (tx - ty)
        return pair_factor.at[
            core, number, pl.ds(pl.multiple_of(row * 8, 8), 8), pl.ds(pl.multiple_of(lane * 128, 128), 128)
        ]

    own_pair.wait()
    for offset in PLANE:
        target = in_plane(offset)
        send(tile_of(target), first.at[p], first_sem, (z, target), 0)
    local(tile_of(p), first.at[p], first_sem)

    send(tiles_hbm, tiles_v.at[core], pair_sem.at[0], partner, 5)
    send(pair_factor.at[core], pair_factor.at[core], pair_sem.at[1], partner, 6)

    def keep_of(number, row_block):
        listed = anc_ref[number, 0] == row_block
        for entry in range(1, anc_ref.shape[1]):
            listed = jnp.logical_or(listed, anc_ref[number, entry] == row_block)
        return jnp.where(listed, jnp.float32(1), jnp.float32(0))

    own_anc.wait()
    keep_low = keep_of(core, 2 * z)
    keep_high = keep_of(core, 2 * z + 1)
    keep0 = keep_of(0, block)
    keep1 = keep_of(1, block)

    own_tiles.wait()

    def split_tiles(half):
        def go(step, carry):
            at = pl.ds(pl.multiple_of(step * 32, 32), 32)
            high, low = split(tiles_v[half, at, :])
            put = pl.ds(pl.multiple_of(half * 256 + step * 32, 32), 32)
            tiles_hi[put, :] = high
            tiles_lo[put, :] = low
            return carry

        lax.fori_loop(0, 8, go, 0)

    split_tiles(core)
    own_link.wait()
    own_dinv0.wait()
    own_dinv1.wait()

    def split_link(step, carry):
        at = pl.ds(pl.multiple_of(step * 32, 32), 32)
        high, low = split(link_v[at, :])
        link_hi[at, :] = high
        link_lo[at, :] = low
        return carry

    lax.fori_loop(0, 16, split_link, 0)

    row_ids = lax.broadcasted_iota(jnp.int32, (16, 512), 0) + p * 16
    col_ids = lax.broadcasted_iota(jnp.int32, (16, 512), 1)
    pick = jnp.where(row_ids == col_ids, jnp.float32(1), jnp.float32(0)).astype(BF16)
    across = (((1,), (1,)), ((), ()))
    picked = lax.dot_general(pick, link_hi[...], across, preferred_element_type=F32) + lax.dot_general(
        pick, link_lo[...], across, preferred_element_type=F32
    )
    picked = dot3(split(picked), split(dinv0_v[...]))
    extra[0] = dot3(split(picked), (link_hi[...], link_lo[...]))
    extra[1] = dot3(split(dinv1_v[0]), (link_hi[...], link_lo[...]))

    wait_bytes(first, first_sem)
    mine = factor_z.at[a, b, :, z]
    for step in RING8:
        dest_z = lax.rem(z + step, 8)
        send(first.at[pl.ds(4 * dest_z, 4)], mine, spread_sem, (dest_z, p), 1)
    local(first.at[pl.ds(4 * z, 4)], mine, spread_sem)

    wait_bytes(tiles_v.at[1 - core], pair_sem.at[0])
    split_tiles(1 - core)

    wait_bytes(pair_factor.at[1 - core], pair_sem.at[1])

    def own_rows(number, keep):
        return jnp.concatenate([pair_factor[0, number], pair_factor[1, number]], axis=0) * keep

    masked0 = own_rows(0, keep0)
    masked1 = own_rows(1, keep1)
    link_pair = (link_hi[...], link_lo[...])
    linked0 = dot3(split(masked0), link_pair)

    def put(buffer, segment, terms):
        for number, term in enumerate(terms):
            at = segment * 192 + number * 64
            buffer[at:at + 64, :] = term

    def put_left(segment, value):
        high, low = split(value)
        put(left_buf, segment, (high, high, low))

    half_cols = pl.ds(pl.multiple_of(core * 256, 256), 256)

    def put_right(segments, number):
        high, low = split(total[number, :, half_cols])
        for segment in segments:
            put(right_buf, segment, (high, low, high))

    total[3] = masked1
    put_left(0, -masked0)
    put_left(2, masked1)
    put_left(4, -linked0)
    put_right((2, 4), 3)

    def piece(lane, row):
        return factor_z.at[lane, row]

    def half(lane, row, which):
        return factor_z.at[lane, row, pl.ds(2 * which, 2)]

    a_next, a_prev, a_far = lax.rem(a + 1, 4), lax.rem(a + 3, 4), lax.rem(a + 2, 4)
    b_next, b_prev, b_far = lax.rem(b + 1, 4), lax.rem(b + 3, 4), lax.rem(b + 2, 4)
    to_b_next, to_b_prev = device(z, a, b_next), device(z, a, b_prev)
    to_a_next, to_a_prev = device(z, a_next, b), device(z, a_prev, b)

    def along_a(row, order):
        send(piece(a, row), piece(a, row), two_sem.at[0, order], to_a_next, 8)
        send(piece(a, row), piece(a, row), two_sem.at[1, order], to_a_prev, 8)

    wait_bytes(piece(a, b), spread_sem)
    send(piece(a, b), piece(a, b), one_sem.at[0], to_b_next, 7)
    send(piece(a, b), piece(a, b), one_sem.at[1], to_b_prev, 7)
    send(piece(a, b), piece(a, b), one_sem.at[2], device(z, a, b_far), 13)
    along_a(b, 0)
    row_order = (b, b_prev, b_next, b_far)

    def relay(order):
        row = row_order[order]
        wait_bytes(piece(a_prev, row), two_sem.at[0, order])
        send(half(a_prev, row, 0), half(a_prev, row, 0), far_sem, to_a_next, 8)
        wait_bytes(piece(a_next, row), two_sem.at[1, order])
        send(half(a_next, row, 1), half(a_next, row, 1), far_sem, to_a_prev, 8)

    wait_bytes(piece(a, b_prev), one_sem.at[0])
    along_a(b_prev, 1)
    wait_bytes(piece(a, b_next), one_sem.at[1])
    along_a(b_next, 2)
    relay(0)
    wait_bytes(piece(a, b_far), one_sem.at[2])
    along_a(b_far, 3)
    send(piece(a, b_far), piece(a, b_far), far_sem, device(z, a_far, b), 8)
    relay(1)

    def compute(number, lane):
        def prepare(step, carry):
            value = jnp.stack([factor_z[lane, row, step] for row in range(4)], axis=1).reshape(256, 128)
            value = value * jnp.where(step < 2, keep_low, keep_high)
            high, low = split(value)
            at = pl.ds(pl.multiple_of(step * 256, 256), 256)
            factor_split[at, 0:128] = high
            factor_split[at, 128:256] = low
            return carry

        lax.fori_loop(0, 4, prepare, 0)

        def multiply(step, carry):
            at = pl.ds(pl.multiple_of(step * 256, 256), 256)
            both = dot(tiles_hi[at, :], factor_split[...])
            result = both[:, 0:128] + both[:, 128:256] + dot(tiles_lo[at, :], factor_split[:, 0:128])
            part[number, :, step] = result.reshape(8, 32, 128)
            return carry

        lax.fori_loop(0, 2, multiply, 0)

    def publish(number, lane, value):
        rows[core, lane] = value.reshape(64, 128)
        send(rows.at[core, lane], rows.at[core, lane], rows_sem, partner, 10)

    def along(distance):
        return lax.rem(z + 8 + (1 - 2 * core) * distance, 8)

    def pair_send(number, slot, dest, to):
        send(
            part.at[number, along(dest)], arrive.at[number, slot], ring_sem.at[number, min(slot, 3)], (along(to), p), 9
        )

    def pairs_start(number):
        pair_send(number, 0, 4, 1)
        pair_send(number, 1, 2, 1)
        pair_send(number, 2, -3, -1)
        pair_send(number, 3, -1, -1)

    def pairs_middle(number):
        for slot, dest in ((0, 3), (2, -2), (1, 1)):
            wait_bytes(arrive.at[number, slot], ring_sem.at[number, slot])
            part[number, along(dest)] = part[number, along(dest)] + arrive[number, slot]
            pair_send(number, slot + 4, dest, dest)

    def pairs_end(number, lane):
        wait_bytes(arrive.at[number, pl.ds(3, 4)], ring_sem.at[number, 3])
        value = part[number, z]
        for slot in range(3, 7):
            value = value + arrive[number, slot]
        publish(number, lane, value)

    compute(0, a)
    pairs_start(0)
    relay(2)
    pairs_middle(0)
    wait_bytes(piece(a_prev, b_far), two_sem.at[0, 3])
    wait_bytes(piece(a_next, b_far), two_sem.at[1, 3])
    compute(1, a_prev)
    pairs_start(1)
    compute(2, a_next)
    pairs_start(2)
    pairs_end(0, a)
    wait_bytes(factor_z.at[a_far], far_sem)
    compute(3, a_far)
    pairs_start(3)
    pairs_middle(1)
    pairs_middle(2)
    pairs_middle(3)
    pairs_end(1, a_prev)
    pairs_end(2, a_next)
    pairs_end(3, a_far)
    wait_bytes(rows.at[1 - core], rows_sem)

    def joined(number):
        return jnp.concatenate([rows[number, lane] for lane in range(4)], axis=1)

    flip = (((0,), (0,)), ((), ()))

    def product(mat, left_segment, right_segment, segments, swap):
        def go(step, carry):
            lanes = pl.ds(pl.multiple_of(step * 256, 256), 256)
            value = lax.dot_general(
                left_buf[left_segment * 192:(left_segment + segments) * 192, lanes],
                right_buf[right_segment * 192:(right_segment + segments) * 192, :],
                flip, preferred_element_type=F32,
            )
            for number in range(8):
                line_x = 2 * step + number // 4
                line_y = number % 4
                upper = line_x + swap * (line_y - line_x)
                lower = line_y + swap * (line_x - line_y)
                gram[mat, upper, lower] = value[number * 32:(number + 1) * 32, :]
            return carry

        lax.fori_loop(0, 2, go, 0)

    own_first = (a, b, a)
    own_second = (b, a, b)
    next_first = (to_a_next, to_b_next, to_a_next)
    prev_first = (to_a_prev, to_b_prev, to_a_prev)

    def gram_start(mat):
        up = lax.rem(own_first[mat] + 1, 4)
        down = lax.rem(own_first[mat] + 3, 4)
        far = lax.rem(own_first[mat] + 2, 4)
        low, high = pl.ds(0, 2), pl.ds(2, 2)
        send(gram.at[mat, far, low], gram_in.at[mat, 0], gram_sem.at[mat, 0], next_first[mat], 11)
        send(gram.at[mat, far, high], gram_in.at[mat, 1], gram_sem.at[mat, 1], prev_first[mat], 11)
        send(gram.at[mat, up, high], gram_in.at[mat, 2], gram_sem.at[mat, 2], next_first[mat], 11)
        send(gram.at[mat, down, low], gram_in.at[mat, 3], gram_sem.at[mat, 2], prev_first[mat], 11)

    def gram_middle(mat):
        up = lax.rem(own_first[mat] + 1, 4)
        down = lax.rem(own_first[mat] + 3, 4)
        low, high = pl.ds(0, 2), pl.ds(2, 2)
        wait_bytes(gram_in.at[mat, 0], gram_sem.at[mat, 0])
        gram[mat, up, low] = gram[mat, up, low] + gram_in[mat, 0]
        send(gram.at[mat, up, low], gram_in.at[mat, 4], gram_sem.at[mat, 2], next_first[mat], 11)
        wait_bytes(gram_in.at[mat, 1], gram_sem.at[mat, 1])
        gram[mat, down, high] = gram[mat, down, high] + gram_in[mat, 1]
        send(gram.at[mat, down, high], gram_in.at[mat, 5], gram_sem.at[mat, 2], prev_first[mat], 11)

    def gram_end(mat):
        here = own_first[mat]
        low, high = pl.ds(0, 2), pl.ds(2, 2)
        wait_bytes(gram_in.at[mat, pl.ds(2, 4)], gram_sem.at[mat, 2])
        line[mat, low] = gram[mat, here, low] + gram_in[mat, 3] + gram_in[mat, 4]
        line[mat, high] = gram[mat, here, high] + gram_in[mat, 2] + gram_in[mat, 5]
        for step in range(1, 4):
            other = lax.rem(own_second[mat] + step, 4)
            target = device(z, a, other) if mat != 1 else device(z, other, b)
            send(line.at[mat, other], line_in.at[mat, step - 1], line_sem.at[mat], target, 12)

    def line_end(mat):
        wait_bytes(line_in.at[mat], line_sem.at[mat])
        value = line[mat, own_second[mat]] + line_in[mat, 0] + line_in[mat, 1] + line_in[mat, 2]
        for row in range(4):
            for lane in range(2):
                plane[2 * row + lane, mat] = value[row * 8:(row + 1) * 8, lane * 128:(lane + 1) * 128]

    off0 = joined(0) * (-keep0)
    total[0] = off0
    put_right((0,), 0)
    product(0, 0, 0, 1, core)
    gram_start(0)

    put_left(1, off0)
    off0_high, off0_low = split(off0)
    both = dot(jnp.concatenate([off0_high, off0_low], axis=0), link_hi[...])
    shifted = both[0:64] + both[64:128] + dot(off0_high, link_lo[...])
    total[1] = shifted
    put_right((1, 5), 1)
    product(1, 0, 1, 2, 1 - core)
    gram_start(1)

    put_left(3, shifted)
    total[2] = joined(1) + shifted
    put_right((3,), 2)
    product(2, 2, 3, 3, core)
    gram_start(2)

    mine_rows = pl.ds(pl.multiple_of(core * 32, 32), 32)
    out_ref[0:32] = total[0, mine_rows, :]
    out_ref[32:64] = total[2, mine_rows, :] * (-keep1)

    for mat in range(3):
        gram_middle(mat)
    for mat in range(3):
        gram_end(mat)
    for mat in range(3):
        line_end(mat)

    for step in RING8:
        dest_z = lax.rem(z + step, 8)
        send(plane.at[dest_z], z_in.at[z], z_sem, (dest_z, p), 2)
    local(plane.at[z], z_in.at[z], z_sem)
    wait_bytes(z_in, z_sem)
    value = z_in[0]
    for other in range(1, 8):
        value = value + z_in[other]
    plane_total = final.at[8]
    final[8] = value
    owner = z // 4
    slot = lax.rem(z, 4) * 2 + core
    for step in RING8:
        send(plane_total, final.at[slot], final_sem, (lax.rem(z + step, 8), (p // 2) * 2 + owner), 3)

    @pl.when(owner == core)
    def _():
        local(plane_total, final.at[slot], final_sem)

    @pl.when(owner != core)
    def _():
        send(plane_total, final.at[slot], final_sem, partner, 4)

    wait_bytes(final.at[pl.ds(0, 8)], final_sem)

    def slice_of(mat):
        tiles = []
        for row in range(2):
            lanes = [final[(2 * row + lane) * 2 + side, mat] for side in range(2) for lane in range(2)]
            tiles.append(jnp.concatenate(lanes, axis=1))
        return jnp.concatenate(tiles, axis=0)

    out_ref[64:80] = dinv1_v[0] + slice_of(0)
    out_ref[80:96] = dinv1_v[1] + extra[0] + slice_of(2)
    out_ref[96:112] = -(extra[1] + slice_of(1))

    wait_bytes(factor_z.at[0, pl.ds(0, 2)], group_send.at[7])
    wait_bytes(tiles_v.at[0], group_send.at[5])
    wait_bytes(pair_factor.at[0], group_send.at[6])
    wait_bytes(factor_z.at[pl.ds(0, 3)], group_send.at[8])
    wait_bytes(arrive, group_send.at[9])
    wait_bytes(rows.at[0], group_send.at[10])
    wait_bytes(gram_in, group_send.at[11])
    wait_bytes(line_in, group_send.at[12])
    wait_bytes(factor_z.at[0, 0], group_send.at[13])
    wait_bytes(first.at[pl.ds(0, 31)], group_send.at[0])
    wait_bytes(first.at[pl.ds(0, 28)], group_send.at[1])
    wait_bytes(plane.at[pl.ds(0, 7)], group_send.at[2])
    wait_bytes(plane.at[pl.ds(0, 7)], group_send.at[3])

    @pl.when(owner != core)
    def _():
        wait_bytes(plane.at[0], group_send.at[4])


def part_out(all_ref, off_ref, diag_ref, link_ref, sems):
    copies = []
    at = 0
    for ref in (off_ref, diag_ref, link_ref):
        for number in range(ref.shape[0]):
            rows = ref.shape[1]
            copies.append(pltpu.make_async_copy(all_ref.at[at:at + rows], ref.at[number], sems.at[len(copies)]))
            at += rows
    for copy in copies:
        copy.start()
    for copy in copies:
        copy.wait()


def body(inverse_tiles, factor, link_factor, diag_inverse, ancestors):
    anywhere = pl.BlockSpec(memory_space=pltpu.MemorySpace.HBM)
    vmem = pl.BlockSpec(memory_space=pltpu.VMEM)
    dma = pltpu.SemaphoreType.DMA
    out = pl.pallas_call(
        kernel,
        out_shape=jax.ShapeDtypeStruct((112, 512), F32),
        in_specs=[anywhere] * 5,
        out_specs=vmem,
        scratch_shapes=[
            pltpu.SMEM((2, 8), jnp.int32),
            pltpu.VMEM((2, 256, 1024), F32),
            pltpu.VMEM((512, 1024), BF16),
            pltpu.VMEM((512, 1024), BF16),
            pltpu.VMEM((32, 8, 128), F32),
            pltpu.VMEM((4, 4, 4, 8, 8, 128), F32),
            pltpu.VMEM((1024, 256), BF16),
            pltpu.VMEM((CHUNKS, 8, 2, 32, 128), F32),
            pltpu.VMEM((CHUNKS, 7, 2, 32, 128), F32),
            pltpu.VMEM((2, 4, 64, 128), F32),
            pltpu.VMEM((2, 2, 32, 512), F32),
            pltpu.VMEM((512, 512), F32),
            pltpu.VMEM((512, 512), BF16),
            pltpu.VMEM((512, 512), BF16),
            pltpu.VMEM((512, 512), F32),
            pltpu.VMEM((2, 16, 512), F32),
            pltpu.VMEM((2, 16, 512), F32),
            pltpu.VMEM((960, 512), BF16),
            pltpu.VMEM((1152, 256), BF16),
            pltpu.VMEM((3, 4, 4, 32, 256), F32),
            pltpu.VMEM((3, 6, 2, 32, 256), F32),
            pltpu.VMEM((3, 4, 32, 256), F32),
            pltpu.VMEM((3, 3, 32, 256), F32),
            pltpu.VMEM((8, 3, 8, 128), F32),
            pltpu.VMEM((8, 3, 8, 128), F32),
            pltpu.VMEM((4, 64, 512), F32),
            pltpu.VMEM((9, 3, 8, 128), F32),
            dma((6,)),
            dma,
            dma,
            dma((2,)),
            dma((3,)),
            dma((2, 4)),
            dma,
            dma((CHUNKS, 4)),
            dma,
            dma((3, 3)),
            dma((3,)),
            dma,
            dma,
            dma((14,)),
        ],
        compiler_params=pltpu.CompilerParams(
            collective_id=0, has_side_effects=True, vmem_limit_bytes=67043328
        ),
    )(inverse_tiles, factor, link_factor, diag_inverse, ancestors)
    return pl.pallas_call(
        part_out,
        out_shape=(
            jax.ShapeDtypeStruct((2, 32, 512), F32),
            jax.ShapeDtypeStruct((2, 16, 512), F32),
            jax.ShapeDtypeStruct((1, 16, 512), F32),
        ),
        in_specs=[vmem],
        out_specs=(anywhere, anywhere, anywhere),
        scratch_shapes=[dma((5,))],
    )(out)


def solution(mesh):
    in_specs = (P("pcol", "prow"), P(None, ("pcol", "prow"), None), P(), P(), P())
    out_specs = (P(None, ("pcol", "prow"), None), P(None, "pcol", None), P(None, "pcol", None))
    return jax.shard_map(body, mesh=mesh, in_specs=in_specs, out_specs=out_specs, check_vma=False)
```

```python
import functools

import jax
import jax.numpy as jnp
from jax import lax
from jax.experimental import pallas as pl
from jax.experimental.pallas import tpu as pltpu
from jax.sharding import PartitionSpec as P

MESH = pl.DeviceIdType.MESH
F32 = jnp.float32
BF16 = jnp.bfloat16
CHUNKS = 4
RING8 = (4, 3, 5, 2, 6, 1, 7)
PLANE = sorted(
    ((dx, dy, dc) for dx in range(4) for dy in range(4) for dc in range(2) if dx or dy or dc),
    key=lambda at: -(min(at[0], 4 - at[0]) + min(at[1], 4 - at[1]) + 0.5 * at[2]),
)


def split(value):
    high = value.astype(BF16)
    low = (value - high.astype(F32)).astype(BF16)
    return high, low


def dot(left, right):
    return jnp.dot(left, right, preferred_element_type=F32)


def dot3(left, right):
    left_high, left_low = left
    right_high, right_low = right
    return dot(left_high, right_high) + dot(left_high, right_low) + dot(left_low, right_high)


def kernel(
    tiles_hbm, factor_hbm, link_hbm, dinv_hbm, anc_hbm,
    out_ref,
    anc_ref, tiles_v, tiles_hi, tiles_lo, first, factor_z, factor_split, part, arrive, rows, pair_factor,
    link_v, link_hi, link_lo, dinv0_v, dinv1_v, extra,
    left_buf, right_buf, gram, gram_in, line, line_in, plane, z_in, total, final,
    local_sem, first_sem, spread_sem, pair_sem, one_sem, two_sem, far_sem, ring_sem, rows_sem,
    gram_sem, line_sem, z_sem, final_sem, group_send,
):
    z = lax.axis_index("prow")
    p = lax.axis_index("pcol")
    core = lax.rem(p, 2)
    x = p // 8
    y = lax.rem(p // 2, 4)
    a = x + core * (y - x)
    b = y + core * (x - y)
    block = p // 2

    def device(dest_z, dest_a, dest_b):
        dest_x = dest_a + core * (dest_b - dest_a)
        dest_y = dest_b + core * (dest_a - dest_b)
        return (dest_z, (dest_x * 4 + dest_y) * 2 + core)

    def local(src, dst, sem):
        copy = pltpu.make_async_copy(src, dst, sem)
        copy.start()
        return copy

    def send(src, dst, recv, target, group):
        pltpu.make_async_remote_copy(
            src_ref=src, dst_ref=dst, send_sem=group_send.at[group], recv_sem=recv,
            device_id=target, device_id_type=MESH,
        ).start()

    def wait_bytes(ref, sem):
        pltpu.make_async_copy(ref, ref, sem).wait()

    own_pair = local(factor_hbm, pair_factor.at[core], local_sem.at[4])
    own_anc = local(anc_hbm, anc_ref, local_sem.at[5])
    own_tiles = local(tiles_hbm, tiles_v.at[core], local_sem.at[0])
    own_link = local(link_hbm.at[0], link_v, local_sem.at[1])
    own_dinv0 = local(dinv_hbm.at[0], dinv0_v, local_sem.at[2])
    slice_rows = pl.ds(pl.multiple_of(p * 16, 16), 16)
    own_dinv1 = local(dinv_hbm.at[:, slice_rows], dinv1_v, local_sem.at[3])

    barrier = pltpu.get_barrier_semaphore()
    def in_plane(offset):
        dx, dy, dc = offset
        return lax.rem(x + dx, 4) * 8 + lax.rem(y + dy, 4) * 2 + (1 - core if dc else core)

    for offset in PLANE:
        pl.semaphore_signal(barrier, inc=1, device_id=(z, in_plane(offset)), device_id_type=MESH)
    for step in RING8:
        pl.semaphore_signal(barrier, inc=1, device_id=(lax.rem(z + step, 8), p), device_id_type=MESH)
    pl.semaphore_wait(barrier, 31 + 7)

    partner = (z, p + 1 - 2 * core)

    def tile_of(target):
        number = lax.rem(target, 2)
        tx = target // 8
        ty = lax.rem(target // 2, 4)
        lane = tx + number * (ty - tx)
        row = ty + number * (tx - ty)
        return pair_factor.at[
            core, number, pl.ds(pl.multiple_of(row * 8, 8), 8), pl.ds(pl.multiple_of(lane * 128, 128), 128)
        ]

    own_pair.wait()
    for offset in PLANE:
        target = in_plane(offset)
        send(tile_of(target), first.at[p], first_sem, (z, target), 0)
    local(tile_of(p), first.at[p], first_sem)

    send(tiles_hbm, tiles_v.at[core], pair_sem.at[0], partner, 5)
    send(pair_factor.at[core], pair_factor.at[core], pair_sem.at[1], partner, 6)

    def keep_of(number, row_block):
        listed = anc_ref[number, 0] == row_block
        for entry in range(1, anc_ref.shape[1]):
            listed = jnp.logical_or(listed, anc_ref[number, entry] == row_block)
        return jnp.where(listed, jnp.float32(1), jnp.float32(0))

    own_anc.wait()
    keep_low = keep_of(core, 2 * z)
    keep_high = keep_of(core, 2 * z + 1)
    keep0 = keep_of(0, block)
    keep1 = keep_of(1, block)

    own_tiles.wait()

    def split_tiles(half):
        def go(step, carry):
            at = pl.ds(pl.multiple_of(step * 32, 32), 32)
            high, low = split(tiles_v[half, at, :])
            put = pl.ds(pl.multiple_of(half * 256 + step * 32, 32), 32)
            tiles_hi[put, :] = high
            tiles_lo[put, :] = low
            return carry

        lax.fori_loop(0, 8, go, 0)

    split_tiles(core)
    own_link.wait()
    own_dinv0.wait()
    own_dinv1.wait()

    def split_link(step, carry):
        at = pl.ds(pl.multiple_of(step * 32, 32), 32)
        high, low = split(link_v[at, :])
        link_hi[at, :] = high
        link_lo[at, :] = low
        return carry

    lax.fori_loop(0, 16, split_link, 0)

    row_ids = lax.broadcasted_iota(jnp.int32, (16, 512), 0) + p * 16
    col_ids = lax.broadcasted_iota(jnp.int32, (16, 512), 1)
    pick = jnp.where(row_ids == col_ids, jnp.float32(1), jnp.float32(0)).astype(BF16)
    across = (((1,), (1,)), ((), ()))
    picked = lax.dot_general(pick, link_hi[...], across, preferred_element_type=F32) + lax.dot_general(
        pick, link_lo[...], across, preferred_element_type=F32
    )
    picked = dot3(split(picked), split(dinv0_v[...]))
    extra[0] = dot3(split(picked), (link_hi[...], link_lo[...]))
    extra[1] = dot3(split(dinv1_v[0]), (link_hi[...], link_lo[...]))

    wait_bytes(first, first_sem)
    mine = factor_z.at[a, b, :, z]
    for step in RING8:
        dest_z = lax.rem(z + step, 8)
        send(first.at[pl.ds(4 * dest_z, 4)], mine, spread_sem, (dest_z, p), 1)
    local(first.at[pl.ds(4 * z, 4)], mine, spread_sem)

    wait_bytes(tiles_v.at[1 - core], pair_sem.at[0])
    split_tiles(1 - core)

    wait_bytes(pair_factor.at[1 - core], pair_sem.at[1])

    def own_rows(number, keep):
        return jnp.concatenate([pair_factor[0, number], pair_factor[1, number]], axis=0) * keep

    masked0 = own_rows(0, keep0)
    masked1 = own_rows(1, keep1)
    link_pair = (link_hi[...], link_lo[...])
    linked0 = dot3(split(masked0), link_pair)

    def put(buffer, segment, terms):
        for number, term in enumerate(terms):
            at = segment * 192 + number * 64
            buffer[at:at + 64, :] = term

    def put_left(segment, value):
        high, low = split(value)
        put(left_buf, segment, (high, high, low))

    half_cols = pl.ds(pl.multiple_of(core * 256, 256), 256)

    def put_right(segments, number):
        high, low = split(total[number, :, half_cols])
        for segment in segments:
            put(right_buf, segment, (high, low, high))

    total[3] = masked1
    put_left(0, -masked0)
    put_left(2, masked1)
    put_left(4, -linked0)
    put_right((2, 4), 3)

    def piece(lane, row):
        return factor_z.at[lane, row]

    def half(lane, row, which):
        return factor_z.at[lane, row, pl.ds(2 * which, 2)]

    a_next, a_prev, a_far = lax.rem(a + 1, 4), lax.rem(a + 3, 4), lax.rem(a + 2, 4)
    b_next, b_prev, b_far = lax.rem(b + 1, 4), lax.rem(b + 3, 4), lax.rem(b + 2, 4)
    to_b_next, to_b_prev = device(z, a, b_next), device(z, a, b_prev)
    to_a_next, to_a_prev = device(z, a_next, b), device(z, a_prev, b)

    def along_a(row, order):
        send(piece(a, row), piece(a, row), two_sem.at[0, order], to_a_next, 8)
        send(piece(a, row), piece(a, row), two_sem.at[1, order], to_a_prev, 8)

    wait_bytes(piece(a, b), spread_sem)
    send(piece(a, b), piece(a, b), one_sem.at[0], to_b_next, 7)
    send(piece(a, b), piece(a, b), one_sem.at[1], to_b_prev, 7)
    send(piece(a, b), piece(a, b), one_sem.at[2], device(z, a, b_far), 13)
    along_a(b, 0)
    row_order = (b, b_prev, b_next, b_far)

    def relay(order):
        row = row_order[order]
        wait_bytes(piece(a_prev, row), two_sem.at[0, order])
        send(half(a_prev, row, 0), half(a_prev, row, 0), far_sem, to_a_next, 8)
        wait_bytes(piece(a_next, row), two_sem.at[1, order])
        send(half(a_next, row, 1), half(a_next, row, 1), far_sem, to_a_prev, 8)

    wait_bytes(piece(a, b_prev), one_sem.at[0])
    along_a(b_prev, 1)
    wait_bytes(piece(a, b_next), one_sem.at[1])
    along_a(b_next, 2)
    relay(0)
    wait_bytes(piece(a, b_far), one_sem.at[2])
    along_a(b_far, 3)
    send(piece(a, b_far), piece(a, b_far), far_sem, device(z, a_far, b), 8)
    relay(1)

    def compute(number, lane):
        def prepare(step, carry):
            value = jnp.stack([factor_z[lane, row, step] for row in range(4)], axis=1).reshape(256, 128)
            value = value * jnp.where(step < 2, keep_low, keep_high)
            high, low = split(value)
            at = pl.ds(pl.multiple_of(step * 256, 256), 256)
            factor_split[at, 0:128] = high
            factor_split[at, 128:256] = low
            return carry

        lax.fori_loop(0, 4, prepare, 0)

        both = dot(tiles_hi[...], factor_split[...])
        result = both[:, 0:128] + both[:, 128:256] + dot(tiles_lo[...], factor_split[:, 0:128])
        for upper in range(2):
            part[number, :, upper] = result[upper * 256:(upper + 1) * 256].reshape(8, 32, 128)

    def publish(number, lane, value):
        rows[core, lane] = value.reshape(64, 128)
        send(rows.at[core, lane], rows.at[core, lane], rows_sem, partner, 10)

    def along(distance):
        return lax.rem(z + 8 + (1 - 2 * core) * distance, 8)

    def pair_send(number, slot, dest, to):
        send(
            part.at[number, along(dest)], arrive.at[number, slot], ring_sem.at[number, min(slot, 3)], (along(to), p), 9
        )

    def pairs_start(number):
        pair_send(number, 0, 4, 1)
        pair_send(number, 1, 2, 1)
        pair_send(number, 2, -3, -1)
        pair_send(number, 3, -1, -1)

    def pairs_middle(number):
        for slot, dest in ((0, 3), (2, -2), (1, 1)):
            wait_bytes(arrive.at[number, slot], ring_sem.at[number, slot])
            part[number, along(dest)] = part[number, along(dest)] + arrive[number, slot]
            pair_send(number, slot + 4, dest, dest)

    def pairs_end(number, lane):
        wait_bytes(arrive.at[number, pl.ds(3, 4)], ring_sem.at[number, 3])
        value = part[number, z]
        for slot in range(3, 7):
            value = value + arrive[number, slot]
        publish(number, lane, value)

    compute(0, a)
    pairs_start(0)
    relay(2)
    pairs_middle(0)
    wait_bytes(piece(a_prev, b_far), two_sem.at[0, 3])
    wait_bytes(piece(a_next, b_far), two_sem.at[1, 3])
    compute(1, a_prev)
    pairs_start(1)
    compute(2, a_next)
    pairs_start(2)
    pairs_end(0, a)
    wait_bytes(factor_z.at[a_far], far_sem)
    compute(3, a_far)
    pairs_start(3)
    pairs_middle(1)
    pairs_middle(2)
    pairs_middle(3)
    pairs_end(1, a_prev)
    pairs_end(2, a_next)
    pairs_end(3, a_far)
    wait_bytes(rows.at[1 - core], rows_sem)

    def joined(number):
        return jnp.concatenate([rows[number, lane] for lane in range(4)], axis=1)

    flip = (((0,), (0,)), ((), ()))

    def product(mat, left_segment, right_segment, segments, swap):
        def go(step, carry):
            lanes = pl.ds(pl.multiple_of(step * 256, 256), 256)
            value = lax.dot_general(
                left_buf[left_segment * 192:(left_segment + segments) * 192, lanes],
                right_buf[right_segment * 192:(right_segment + segments) * 192, :],
                flip, preferred_element_type=F32,
            )
            for number in range(8):
                line_x = 2 * step + number // 4
                line_y = number % 4
                upper = line_x + swap * (line_y - line_x)
                lower = line_y + swap * (line_x - line_y)
                gram[mat, upper, lower] = value[number * 32:(number + 1) * 32, :]
            return carry

        lax.fori_loop(0, 2, go, 0)

    own_first = (a, b, a)
    own_second = (b, a, b)
    next_first = (to_a_next, to_b_next, to_a_next)
    prev_first = (to_a_prev, to_b_prev, to_a_prev)

    def gram_start(mat):
        up = lax.rem(own_first[mat] + 1, 4)
        down = lax.rem(own_first[mat] + 3, 4)
        far = lax.rem(own_first[mat] + 2, 4)
        low, high = pl.ds(0, 2), pl.ds(2, 2)
        send(gram.at[mat, far, low], gram_in.at[mat, 0], gram_sem.at[mat, 0], next_first[mat], 11)
        send(gram.at[mat, far, high], gram_in.at[mat, 1], gram_sem.at[mat, 1], prev_first[mat], 11)
        send(gram.at[mat, up, high], gram_in.at[mat, 2], gram_sem.at[mat, 2], next_first[mat], 11)
        send(gram.at[mat, down, low], gram_in.at[mat, 3], gram_sem.at[mat, 2], prev_first[mat], 11)

    def gram_middle(mat):
        up = lax.rem(own_first[mat] + 1, 4)
        down = lax.rem(own_first[mat] + 3, 4)
        low, high = pl.ds(0, 2), pl.ds(2, 2)
        wait_bytes(gram_in.at[mat, 0], gram_sem.at[mat, 0])
        gram[mat, up, low] = gram[mat, up, low] + gram_in[mat, 0]
        send(gram.at[mat, up, low], gram_in.at[mat, 4], gram_sem.at[mat, 2], next_first[mat], 11)
        wait_bytes(gram_in.at[mat, 1], gram_sem.at[mat, 1])
        gram[mat, down, high] = gram[mat, down, high] + gram_in[mat, 1]
        send(gram.at[mat, down, high], gram_in.at[mat, 5], gram_sem.at[mat, 2], prev_first[mat], 11)

    def gram_end(mat):
        here = own_first[mat]
        low, high = pl.ds(0, 2), pl.ds(2, 2)
        wait_bytes(gram_in.at[mat, pl.ds(2, 4)], gram_sem.at[mat, 2])
        line[mat, low] = gram[mat, here, low] + gram_in[mat, 3] + gram_in[mat, 4]
        line[mat, high] = gram[mat, here, high] + gram_in[mat, 2] + gram_in[mat, 5]
        for step in range(1, 4):
            other = lax.rem(own_second[mat] + step, 4)
            target = device(z, a, other) if mat != 1 else device(z, other, b)
            send(line.at[mat, other], line_in.at[mat, step - 1], line_sem.at[mat], target, 12)

    def line_end(mat):
        wait_bytes(line_in.at[mat], line_sem.at[mat])
        value = line[mat, own_second[mat]] + line_in[mat, 0] + line_in[mat, 1] + line_in[mat, 2]
        for row in range(4):
            for lane in range(2):
                plane[2 * row + lane, mat] = value[row * 8:(row + 1) * 8, lane * 128:(lane + 1) * 128]

    off0 = joined(0) * (-keep0)
    total[0] = off0
    put_right((0,), 0)
    product(0, 0, 0, 1, core)
    gram_start(0)

    put_left(1, off0)
    off0_high, off0_low = split(off0)
    both = dot(jnp.concatenate([off0_high, off0_low], axis=0), link_hi[...])
    shifted = both[0:64] + both[64:128] + dot(off0_high, link_lo[...])
    total[1] = shifted
    put_right((1, 5), 1)
    product(1, 0, 1, 2, 1 - core)
    gram_start(1)

    put_left(3, shifted)
    total[2] = joined(1) + shifted
    put_right((3,), 2)
    product(2, 2, 3, 3, core)
    gram_start(2)

    mine_rows = pl.ds(pl.multiple_of(core * 32, 32), 32)
    out_ref[0:32] = total[0, mine_rows, :]
    out_ref[32:64] = total[2, mine_rows, :] * (-keep1)

    for mat in range(3):
        gram_middle(mat)
    for mat in range(3):
        gram_end(mat)
    for mat in range(3):
        line_end(mat)

    for step in RING8:
        dest_z = lax.rem(z + step, 8)
        send(plane.at[dest_z], z_in.at[z], z_sem, (dest_z, p), 2)
    local(plane.at[z], z_in.at[z], z_sem)
    wait_bytes(z_in, z_sem)
    value = z_in[0]
    for other in range(1, 8):
        value = value + z_in[other]
    plane_total = final.at[8]
    final[8] = value
    owner = z // 4
    slot = lax.rem(z, 4) * 2 + core
    for step in RING8:
        send(plane_total, final.at[slot], final_sem, (lax.rem(z + step, 8), (p // 2) * 2 + owner), 3)

    @pl.when(owner == core)
    def _():
        local(plane_total, final.at[slot], final_sem)

    @pl.when(owner != core)
    def _():
        send(plane_total, final.at[slot], final_sem, partner, 4)

    wait_bytes(final.at[pl.ds(0, 8)], final_sem)

    def slice_of(mat):
        tiles = []
        for row in range(2):
            lanes = [final[(2 * row + lane) * 2 + side, mat] for side in range(2) for lane in range(2)]
            tiles.append(jnp.concatenate(lanes, axis=1))
        return jnp.concatenate(tiles, axis=0)

    out_ref[64:80] = dinv1_v[0] + slice_of(0)
    out_ref[80:96] = dinv1_v[1] + extra[0] + slice_of(2)
    out_ref[96:112] = -(extra[1] + slice_of(1))

    wait_bytes(factor_z.at[0, pl.ds(0, 2)], group_send.at[7])
    wait_bytes(tiles_v.at[0], group_send.at[5])
    wait_bytes(pair_factor.at[0], group_send.at[6])
    wait_bytes(factor_z.at[pl.ds(0, 3)], group_send.at[8])
    wait_bytes(arrive, group_send.at[9])
    wait_bytes(rows.at[0], group_send.at[10])
    wait_bytes(gram_in, group_send.at[11])
    wait_bytes(line_in, group_send.at[12])
    wait_bytes(factor_z.at[0, 0], group_send.at[13])
    wait_bytes(first.at[pl.ds(0, 31)], group_send.at[0])
    wait_bytes(first.at[pl.ds(0, 28)], group_send.at[1])
    wait_bytes(plane.at[pl.ds(0, 7)], group_send.at[2])
    wait_bytes(plane.at[pl.ds(0, 7)], group_send.at[3])

    @pl.when(owner != core)
    def _():
        wait_bytes(plane.at[0], group_send.at[4])


def part_out(all_ref, off_ref, diag_ref, link_ref, sems):
    copies = []
    at = 0
    for ref in (off_ref, diag_ref, link_ref):
        for number in range(ref.shape[0]):
            rows = ref.shape[1]
            copies.append(pltpu.make_async_copy(all_ref.at[at:at + rows], ref.at[number], sems.at[len(copies)]))
            at += rows
    for copy in copies:
        copy.start()
    for copy in copies:
        copy.wait()


def body(inverse_tiles, factor, link_factor, diag_inverse, ancestors):
    anywhere = pl.BlockSpec(memory_space=pltpu.MemorySpace.HBM)
    vmem = pl.BlockSpec(memory_space=pltpu.VMEM)
    dma = pltpu.SemaphoreType.DMA
    out = pl.pallas_call(
        kernel,
        out_shape=jax.ShapeDtypeStruct((112, 512), F32),
        in_specs=[anywhere] * 5,
        out_specs=vmem,
        scratch_shapes=[
            pltpu.SMEM((2, 8), jnp.int32),
            pltpu.VMEM((2, 256, 1024), F32),
            pltpu.VMEM((512, 1024), BF16),
            pltpu.VMEM((512, 1024), BF16),
            pltpu.VMEM((32, 8, 128), F32),
            pltpu.VMEM((4, 4, 4, 8, 8, 128), F32),
            pltpu.VMEM((1024, 256), BF16),
            pltpu.VMEM((CHUNKS, 8, 2, 32, 128), F32),
            pltpu.VMEM((CHUNKS, 7, 2, 32, 128), F32),
            pltpu.VMEM((2, 4, 64, 128), F32),
            pltpu.VMEM((2, 2, 32, 512), F32),
            pltpu.VMEM((512, 512), F32),
            pltpu.VMEM((512, 512), BF16),
            pltpu.VMEM((512, 512), BF16),
            pltpu.VMEM((512, 512), F32),
            pltpu.VMEM((2, 16, 512), F32),
            pltpu.VMEM((2, 16, 512), F32),
            pltpu.VMEM((960, 512), BF16),
            pltpu.VMEM((1152, 256), BF16),
            pltpu.VMEM((3, 4, 4, 32, 256), F32),
            pltpu.VMEM((3, 6, 2, 32, 256), F32),
            pltpu.VMEM((3, 4, 32, 256), F32),
            pltpu.VMEM((3, 3, 32, 256), F32),
            pltpu.VMEM((8, 3, 8, 128), F32),
            pltpu.VMEM((8, 3, 8, 128), F32),
            pltpu.VMEM((4, 64, 512), F32),
            pltpu.VMEM((9, 3, 8, 128), F32),
            dma((6,)),
            dma,
            dma,
            dma((2,)),
            dma((3,)),
            dma((2, 4)),
            dma,
            dma((CHUNKS, 4)),
            dma,
            dma((3, 3)),
            dma((3,)),
            dma,
            dma,
            dma((14,)),
        ],
        compiler_params=pltpu.CompilerParams(
            collective_id=0, has_side_effects=True, vmem_limit_bytes=67043328
        ),
    )(inverse_tiles, factor, link_factor, diag_inverse, ancestors)
    return pl.pallas_call(
        part_out,
        out_shape=(
            jax.ShapeDtypeStruct((2, 32, 512), F32),
            jax.ShapeDtypeStruct((2, 16, 512), F32),
            jax.ShapeDtypeStruct((1, 16, 512), F32),
        ),
        in_specs=[vmem],
        out_specs=(anywhere, anywhere, anywhere),
        scratch_shapes=[dma((5,))],
    )(out)


def solution(mesh):
    in_specs = (P("pcol", "prow"), P(None, ("pcol", "prow"), None), P(), P(), P())
    out_specs = (P(None, ("pcol", "prow"), None), P(None, "pcol", None), P(None, "pcol", None))
    return jax.shard_map(body, mesh=mesh, in_specs=in_specs, out_specs=out_specs, check_vma=False)
```
